32 devices in a mesh: dp: 16 (over z, x, core), tensor: 2 (over y).
Axes of the slice: x: 2, y: 2, z: 4, core: 2. Of those that a mesh axis runs over, the one named last changes fastest.
Arguments:
- tokens: bfloat16 [3072, 1536], P('dp'), may hold values from -6 to 6
- prefix: int32 [16], P('dp'), may hold values from 19 to 96
- g_attn: bfloat16 [1536], P('dp'), may hold values from 0.5 to 1.5
- w_query: bfloat16 [128, 12, 1536], P('dp', 'tensor'), may hold values from -0.15625 to 0.15625
- b_query: bfloat16 [128, 12], P('dp', 'tensor'), may hold values from -3 to 3
- w_key: bfloat16 [128, 2, 1536], P('dp', 'tensor'), may hold values from -0.15625 to 0.15625
- b_key: bfloat16 [128, 2], P(None, 'tensor'), may hold values from -3 to 3
- w_value: bfloat16 [128, 2, 1536], P('dp', 'tensor'), may hold values from -0.15625 to 0.15625
- b_value: bfloat16 [128, 2], P('dp', 'tensor'), may hold values from -3 to 3
- w_out: bfloat16 [128, 12, 1536], P('dp', 'tensor'), may hold values from -0.75 to 0.75
- g_mlp: bfloat16 [1536], P('dp'), may hold values from 0.5 to 1.5
- w_gate: bfloat16 [8960, 1536], P(('dp', 'tensor')), may hold values from -0.15625 to 0.15625
- w_up: bfloat16 [8960, 1536], P(('dp', 'tensor')), may hold values from -0.15625 to 0.15625
- w_down: bfloat16 [8960, 1536], P(('dp', 'tensor')), may hold values from -0.0625 to 0.0625
- cotangent: bfloat16 [3072, 1536], P('dp'), may hold values from -6 to 6
Outputs:
- out_tokens: bfloat16 [3072, 1536], P('dp')
- grad_tokens: float32 [3072, 1536], P('dp')
- grad_gattn: float32 [1536], P('dp')
- grad_wquery: float32 [128, 12, 1536], P('dp', 'tensor')
- grad_bquery: float32 [128, 12], P('dp', 'tensor')
- grad_wkey: float32 [128, 2, 1536], P('dp', 'tensor')
- grad_bkey: float32 [128, 2], P(None, 'tensor')
- grad_wvalue: float32 [128, 2, 1536], P('dp', 'tensor')
- grad_bvalue: float32 [128, 2], P('dp', 'tensor')
- grad_wout: float32 [128, 12, 1536], P('dp', 'tensor')
- grad_gmlp: float32 [1536], P('dp')
- grad_wgate: float32 [8960, 1536], P(('dp', 'tensor'))
- grad_wup: float32 [8960, 1536], P(('dp', 'tensor'))
- grad_wdown: float32 [8960, 1536], P(('dp', 'tensor'))
The draws below stay inside these ranges and needn't reach their ends.
All inputs are finite; a program needn't handle non-finite values.
Results may differ from the reference program's by a relative error of at most 0.022.
Values may be sent and summed in bfloat16 or wider, within the bound.
A program may use at most 256 MiB of HBM per device.

```python
import jax
import jax.numpy as jnp
from jax import lax

D = 1536
H = 12
KV = 2
HD = 128
FF = 8960
SEQ = 192
SEQS = 16
TOKENS = 3072


def place_ends(drawn, key, low, high):
    longest = drawn.shape.index(max(drawn.shape))
    spots = []
    for shift in (0, 1):
        where = [jax.random.randint(jax.random.fold_in(key, axis), (), 0, length) for axis, length in enumerate(drawn.shape)]
        where[longest] = (where[longest] + shift) % drawn.shape[longest]
        spots.append(tuple(where))
    return drawn.at[spots[0]].set(low).at[spots[1]].set(high)


def strengthened(values, key, source, target, parts, factor):
    owner, partner = [(jnp.arange(values.shape[dim]) // (values.shape[dim] // parts)).reshape([-1 if axis == dim else 1 for axis in range(values.ndim)]) for dim in (source, target)]
    chosen = jax.random.permutation(key, parts)[partner]
    strong = (owner == chosen) | (owner == (partner + parts // 2) % parts)
    return jnp.where(strong, factor * values, values)


def levels(rng, shape, pieces, low, top_value):
    loudness = 1.0
    for axis_at, blocks in pieces:
        draws = jax.random.uniform(jax.random.fold_in(jax.random.fold_in(rng, 6), axis_at), (blocks,), jnp.float32, low / len(pieces), top_value / len(pieces))
        loudness = loudness * jnp.repeat(jnp.exp(draws), shape[axis_at] // blocks).reshape((-1,) + (1,) * (len(shape) - 1 - axis_at))
    return loudness


def normal_values(key, dims, spread, most, cuts=(), held_as=jnp.bfloat16):
    values = jax.random.normal(key, dims, jnp.float32) * spread
    if len(cuts) > 0:
        values = levels(key, dims, cuts, -0.22, 0.18) * values
    return jnp.clip(values, min=-most, max=most).astype(held_as)


def gaussian_with(stream_key, extent, scale, most, split, heavy, kind=jnp.bfloat16):
    values = scale * jax.random.normal(stream_key, extent, jnp.float32)
    if split:
        values = values * levels(stream_key, extent, split, -0.22, 0.18)
    return jnp.clip(strengthened(values, jax.random.fold_in(stream_key, 3), *heavy), -most, most).astype(kind)


def setup_inputs(seed: int = 0) -> dict:
    keys = jax.random.split(jax.random.key(seed), 16)
    return {
        "tokens": normal_values(keys[0], (TOKENS, D), 1.0, 6.0, ((0, 16),)),
        "prefix": place_ends(jax.random.randint(keys[1], (SEQS,), SEQ // 10, SEQ // 2 + 1), jax.random.fold_in(keys[1], 1), SEQ // 10, (SEQ // 2 + 1) - 1).astype(jnp.int32),
        "g_attn": jnp.clip(1.0 + 0.1 * jax.random.normal(keys[2], (D,), jnp.float32), 0.5, 1.5).astype(jnp.bfloat16),
        "w_query": normal_values(keys[3], (HD, H, D), D ** -0.5, 0.15625, ((0, 16), (1, 2))),
        "b_query": normal_values(keys[4], (HD, H), 0.5, 3.0, ((0, 16), (1, 2))),
        "w_key": normal_values(keys[5], (HD, KV, D), D ** -0.5, 0.15625, ((0, 16), (1, 2))),
        "b_key": normal_values(keys[6], (HD, KV), 0.5, 3.0, ((1, 2),)),
        "w_value": normal_values(keys[7], (HD, KV, D), D ** -0.5, 0.15625, ((0, 16), (1, 2))),
        "b_value": normal_values(keys[8], (HD, KV), 0.5, 3.0, ((0, 16), (1, 2))),
        "w_out": normal_values(keys[9], (HD, H, D), (8 * H * HD // SEQ) ** -0.5, 0.75, ((0, 16), (1, 2))),
        "g_mlp": jnp.clip(1.0 + 0.1 * jax.random.normal(keys[10], (D,), jnp.float32), 0.5, 1.5).astype(jnp.bfloat16),
        "w_gate": normal_values(keys[11], (FF, D), D ** -0.5, 0.15625, ((0, 32),)),
        "w_up": normal_values(keys[12], (FF, D), D ** -0.5, 0.15625, ((0, 32),)),
        "w_down": normal_values(keys[13], (FF, D), FF ** -0.5, 0.0625, ((0, 32),)),
        "cotangent": gaussian_with(keys[14], (TOKENS, D), 1.0, 6.0, ((0, 16),), (0, 1, 16, 2.0)),
    }


EPS = 1e-06
ROPE_BASE = 1000000.0
NEG_BIG = -1e+30
HIGH = lax.Precision.HIGHEST

@jax.custom_vjp
def low(v):
    return lax.optimization_barrier(v.astype(jnp.bfloat16)).astype(jnp.float32)

@jax.custom_vjp
def low_back(v):
    return v

def low_keep(v):
    return (low(v), None)

def low_pass(kept, grad):
    return (grad,)

def back_keep(v):
    return (v, None)

def back_low(kept, grad):
    return (low(grad),)
low.defvjp(low_keep, low_pass)
low_back.defvjp(back_keep, back_low)

def rounded(value):
    return low_back(low(value))

def rotate(field, flip_sign):
    half_dim = field.shape[-1] // 2
    places = jnp.arange(field.shape[0], dtype=jnp.float32)
    freqs = ROPE_BASE ** (-(jnp.arange(half_dim, dtype=jnp.float32) * 2.0 / field.shape[-1]))
    angles = places[:, None] * freqs[None, :]
    cosine = jnp.cos(angles)[:, None, :]
    sine = flip_sign * jnp.sin(angles)[:, None, :]
    first = field[..., :half_dim]
    second = field[..., half_dim:]
    return jnp.concatenate([first * cosine - second * sine, second * cosine + first * sine], axis=-1)

def attend(inputs):
    query_pre, key_pre, value_low, prefix_len = inputs
    seq_len = query_pre.shape[0]
    kv_heads = key_pre.shape[1]
    group_size = query_pre.shape[1] // kv_heads
    head_dim = query_pre.shape[2]
    query_rot = low(rotate(query_pre, 1.0)).reshape(seq_len, kv_heads, group_size, head_dim)
    key_rot = low(rotate(key_pre, 1.0))
    scores = jnp.einsum('skgd,tkd->kgst', query_rot, key_rot, precision=HIGH) * head_dim ** (-0.5)
    scores = low_back(scores)
    row_index = jnp.arange(seq_len)[:, None]
    col_index = jnp.arange(seq_len)[None, :]
    allowed = (col_index <= row_index) | (col_index < prefix_len)
    scores = jnp.where(allowed, scores, NEG_BIG)
    attn_probs = low(jax.nn.softmax(scores, axis=-1))
    mixture = jnp.einsum('kgst,tkd->skgd', attn_probs, value_low, precision=HIGH)
    return mixture.reshape(seq_len, query_pre.shape[1], head_dim)

def forward(tok_float, params, prefix):
    g_attn, w_query, b_query, w_key, b_key, w_value, b_value, w_out, g_mlp, w_gate, w_up, w_down = params
    rms_attn = lax.rsqrt(lax.optimization_barrier(jnp.mean(tok_float * tok_float, axis=-1, keepdims=True)) + EPS)
    normed_in = low(tok_float * rms_attn * g_attn)
    query_pre = low_back(jnp.einsum('sd,ehd->she', normed_in, w_query, precision=HIGH) + b_query.T)
    key_pre = low_back(jnp.einsum('sd,ehd->she', normed_in, w_key, precision=HIGH) + b_key.T)
    value_pre = rounded(jnp.einsum('sd,ehd->she', normed_in, w_value, precision=HIGH) + b_value.T)
    seq_count = tok_float.shape[0] // SEQ
    attended = lax.map(jax.checkpoint(attend), (query_pre.reshape(seq_count, SEQ, H, HD), key_pre.reshape(seq_count, SEQ, KV, HD), value_pre.reshape(seq_count, SEQ, KV, HD), prefix))
    attended = rounded(attended.reshape(-1, H, HD))
    branch = low_back(jnp.einsum('she,ehd->sd', attended, w_out, precision=HIGH))
    middle = tok_float + branch
    rms_mlp = lax.rsqrt(lax.optimization_barrier(jnp.mean(middle * middle, axis=-1, keepdims=True)) + EPS)
    normed_mid = low(middle * rms_mlp * g_mlp)
    gate_val = low_back(jnp.dot(normed_mid, w_gate.T, precision=HIGH))
    up_val = low_back(jnp.dot(normed_mid, w_up.T, precision=HIGH))
    hidden = low(jax.nn.silu(gate_val) * up_val)
    return middle + low_back(jnp.dot(hidden, w_down, precision=HIGH))

def reference(tokens, prefix, g_attn, w_query, b_query, w_key, b_key, w_value, b_value, w_out, g_mlp, w_gate, w_up, w_down, cotangent):
    params = tuple((array_in.astype(jnp.float32) for array_in in (g_attn, w_query, b_query, w_key, b_key, w_value, b_value, w_out, g_mlp, w_gate, w_up, w_down)))
    group_seqs = max([candidate for candidate in range(1, SEQS + 1) if SEQS % candidate == 0 and candidate * SEQ <= 4096], default=1)
    blocks = SEQS // group_seqs
    tok_blocks = tokens.astype(jnp.float32).reshape(blocks, group_seqs * SEQ, D)
    cot_blocks = cotangent.astype(jnp.float32).reshape(blocks, group_seqs * SEQ, D)
    pre_blocks = prefix.reshape(blocks, group_seqs)

    def one_block(totals, inputs):
        tok_block, cot_block, pre_block = inputs

        def closed(tok_in, params_in):
            return forward(tok_in, params_in, pre_block)
        result, pullback = jax.vjp(closed, tok_block, params)
        grad_in, grad_params = pullback(cot_block)
        totals = jax.tree.map(jnp.add, totals, grad_params)
        return (totals, (result.astype(jnp.bfloat16), grad_in))
    zeros_init = jax.tree.map(jnp.zeros_like, params)
    totals, (outs_seq, grads_seq) = lax.scan(one_block, zeros_init, (tok_blocks, cot_blocks, pre_blocks))
    return (outs_seq.reshape(TOKENS, D), grads_seq.reshape(TOKENS, D), totals[0], totals[1], totals[2], totals[3], totals[4], totals[5], totals[6], totals[7], totals[8], totals[9], totals[10], totals[11])
```

```python
import functools

import jax
import jax.numpy as jnp
from jax import lax
from jax.experimental import pallas as pl
from jax.experimental.pallas import tpu as pltpu
from jax.sharding import PartitionSpec as P

EPS = 1e-06
ROPE_BASE = 1000000.0
NEG_BIG = -1e30


def rotate(field, flip_sign):
    half_dim = field.shape[-1] // 2
    places = jnp.arange(field.shape[0], dtype=jnp.float32)
    freqs = ROPE_BASE ** (-(jnp.arange(half_dim, dtype=jnp.float32) * 2.0 / field.shape[-1]))
    angles = places[:, None] * freqs[None, :]
    cosine = jnp.cos(angles)[:, None, :]
    sine = flip_sign * jnp.sin(angles)[:, None, :]
    first = field[..., :half_dim]
    second = field[..., half_dim:]
    return jnp.concatenate(
        [first * cosine - second * sine, second * cosine + first * sine], axis=-1
    )


def normed(field, gain):
    return field * lax.rsqrt(jnp.mean(field * field, axis=-1, keepdims=True) + EPS) * gain


def whole_gather(
    tokens,
    prefix,
    g_attn,
    w_query,
    b_query,
    w_key,
    b_key,
    w_value,
    b_value,
    w_out,
    g_mlp,
    w_gate,
    w_up,
    w_down,
    cotangent,
):
    gain_one, query_w, query_b, key_w, value_w, value_b, out_w = (
        lax.all_gather(g_attn, "dp", axis=0, tiled=True),
        lax.all_gather(w_query, "dp", axis=0, tiled=True),
        lax.all_gather(b_query, "dp", axis=0, tiled=True),
        lax.all_gather(w_key, "dp", axis=0, tiled=True),
        lax.all_gather(w_value, "dp", axis=0, tiled=True),
        lax.all_gather(b_value, "dp", axis=0, tiled=True),
        lax.all_gather(w_out, "dp", axis=0, tiled=True),
    )
    tok_float = tokens.astype(jnp.float32)
    gain_in = gain_one.astype(jnp.float32)
    normed_in = normed(tok_float, gain_in).astype(jnp.bfloat16)
    query_pre = (
        jnp.einsum("sd,ehd->she", normed_in, query_w, preferred_element_type=jnp.float32)
        + query_b.astype(jnp.float32).T
    )
    key_pre = (
        jnp.einsum("sd,ehd->she", normed_in, key_w, preferred_element_type=jnp.float32)
        + b_key.astype(jnp.float32).T
    )
    value_pre = (
        jnp.einsum("sd,ehd->she", normed_in, value_w, preferred_element_type=jnp.float32)
        + value_b.astype(jnp.float32).T
    )
    seq_len, heads_local, head_dim = query_pre.shape
    kv_local = key_pre.shape[1]
    group_size = heads_local // kv_local
    score_scale = head_dim ** (-0.5)
    query_rot = (
        rotate(query_pre, 1.0).astype(jnp.bfloat16).reshape(seq_len, kv_local, group_size, head_dim)
    )
    key_rot = rotate(key_pre, 1.0).astype(jnp.bfloat16)
    value_low = value_pre.astype(jnp.bfloat16)
    row_index = lax.broadcasted_iota(jnp.int32, (seq_len, seq_len), 0)
    col_index = lax.broadcasted_iota(jnp.int32, (seq_len, seq_len), 1)
    allowed = (col_index <= row_index) | (col_index < prefix[0])

    def score_of():
        raw_scores = (
            jnp.einsum("skgd,tkd->kgst", query_rot, key_rot, preferred_element_type=jnp.float32)
            * score_scale
        )
        return jnp.where(allowed, raw_scores, NEG_BIG)

    scores = score_of()
    row_peak = jnp.max(scores, axis=-1, keepdims=True)
    shifted_exp = jnp.exp(scores - row_peak)
    row_total = jnp.sum(shifted_exp, axis=-1, keepdims=True)
    probs_low = (shifted_exp / row_total).astype(jnp.bfloat16)
    log_total = row_peak + jnp.log(row_total)
    attended = jnp.einsum(
        "kgst,tkd->skgd", probs_low, value_low, preferred_element_type=jnp.float32
    )
    attended_low = attended.reshape(seq_len, heads_local, head_dim).astype(jnp.bfloat16)
    attn_part = jnp.einsum("she,ehd->sd", attended_low, out_w, preferred_element_type=jnp.float32)
    middle = tok_float + lax.psum(attn_part, "tensor")
    gain_two, gate_w, up_w, down_w = (
        lax.all_gather(g_mlp, "dp", axis=0, tiled=True),
        lax.all_gather(w_gate, "dp", axis=0, tiled=True),
        lax.all_gather(w_up, "dp", axis=0, tiled=True),
        lax.all_gather(w_down, "dp", axis=0, tiled=True),
    )
    gain_mid = gain_two.astype(jnp.float32)
    normed_mid = normed(middle, gain_mid).astype(jnp.bfloat16)
    contract = (((1,), (1,)), ((), ()))
    rows_first = (((0,), (0,)), ((), ()))
    gate_val = lax.dot_general(normed_mid, gate_w, contract, preferred_element_type=jnp.float32)
    up_val = lax.dot_general(normed_mid, up_w, contract, preferred_element_type=jnp.float32)
    sigmoid_gate = jax.nn.sigmoid(gate_val)
    silu_gate = gate_val * sigmoid_gate
    hidden = (silu_gate * up_val).astype(jnp.bfloat16)
    mlp_part = jnp.dot(hidden, down_w, preferred_element_type=jnp.float32)
    result = middle + lax.psum(mlp_part.astype(jnp.bfloat16), "tensor").astype(jnp.float32)
    out_tokens = result.astype(jnp.bfloat16)
    gain_two, gate_w, up_w, down_w = (
        lax.all_gather(g_mlp, "dp", axis=0, tiled=True),
        lax.all_gather(w_gate, "dp", axis=0, tiled=True),
        lax.all_gather(w_up, "dp", axis=0, tiled=True),
        lax.all_gather(w_down, "dp", axis=0, tiled=True),
    )
    cot_float = cotangent.astype(jnp.float32)
    grad_wdown = lax.dot_general(hidden, cotangent, rows_first, preferred_element_type=jnp.float32)
    grad_hidden = lax.dot_general(cotangent, down_w, contract, preferred_element_type=jnp.float32)
    grad_gate = (
        grad_hidden * up_val * sigmoid_gate * (1.0 + gate_val * (1.0 - sigmoid_gate))
    ).astype(jnp.bfloat16)
    grad_up = (grad_hidden * silu_gate).astype(jnp.bfloat16)
    grad_wgate = lax.dot_general(
        grad_gate, normed_mid, rows_first, preferred_element_type=jnp.float32
    )
    grad_wup = lax.dot_general(grad_up, normed_mid, rows_first, preferred_element_type=jnp.float32)
    mid_part = jnp.dot(grad_gate, gate_w, preferred_element_type=jnp.float32) + jnp.dot(
        grad_up, up_w, preferred_element_type=jnp.float32
    )
    grad_normed_mid = lax.psum(mid_part, "tensor")
    unused_mid, pull_mid = jax.vjp(normed, middle, gain_mid)
    grad_mid_norm, grad_gmlp = pull_mid(grad_normed_mid)
    grad_middle = cot_float + grad_mid_norm
    gain_one, query_w, query_b, key_w, value_w, value_b, out_w = (
        lax.all_gather(g_attn, "dp", axis=0, tiled=True),
        lax.all_gather(w_query, "dp", axis=0, tiled=True),
        lax.all_gather(b_query, "dp", axis=0, tiled=True),
        lax.all_gather(w_key, "dp", axis=0, tiled=True),
        lax.all_gather(w_value, "dp", axis=0, tiled=True),
        lax.all_gather(b_value, "dp", axis=0, tiled=True),
        lax.all_gather(w_out, "dp", axis=0, tiled=True),
    )
    middle_low = grad_middle.astype(jnp.bfloat16)
    grad_wout = jnp.einsum(
        "she,sd->ehd", attended_low, middle_low, preferred_element_type=jnp.float32
    )
    grad_attended = (
        jnp.einsum("sd,ehd->she", middle_low, out_w, preferred_element_type=jnp.float32)
        .astype(jnp.bfloat16)
        .reshape(seq_len, kv_local, group_size, head_dim)
    )
    probs_again = jnp.exp(score_of() - log_total)
    again_low = probs_again.astype(jnp.bfloat16)
    grad_value = jnp.einsum(
        "kgst,skgd->tkd", again_low, grad_attended, preferred_element_type=jnp.float32
    ).astype(jnp.bfloat16)
    grad_probs = jnp.einsum(
        "skgd,tkd->kgst", grad_attended, value_low, preferred_element_type=jnp.float32
    )
    inner_sum = jnp.sum(probs_again * grad_probs, axis=-1, keepdims=True)
    grad_scores = (probs_again * (grad_probs - inner_sum)).astype(jnp.bfloat16)
    grad_qrot = (
        jnp.einsum(
            "kgst,tkd->skgd", grad_scores, key_rot, preferred_element_type=jnp.float32
        ).reshape(seq_len, heads_local, head_dim)
        * score_scale
    )
    grad_krot = (
        jnp.einsum("kgst,skgd->tkd", grad_scores, query_rot, preferred_element_type=jnp.float32)
        * score_scale
    )
    grad_query = rotate(grad_qrot, -1.0).astype(jnp.bfloat16)
    grad_key = rotate(grad_krot, -1.0).astype(jnp.bfloat16)
    grad_wquery = jnp.einsum(
        "she,sd->ehd", grad_query, normed_in, preferred_element_type=jnp.float32
    )
    grad_bquery = jnp.sum(grad_query.astype(jnp.float32), axis=0).T
    grad_wkey = jnp.einsum("she,sd->ehd", grad_key, normed_in, preferred_element_type=jnp.float32)
    grad_bkey = jnp.sum(grad_key.astype(jnp.float32), axis=0).T
    key_bias_total = lax.psum(grad_bkey, "dp")
    grad_wvalue = jnp.einsum(
        "she,sd->ehd", grad_value, normed_in, preferred_element_type=jnp.float32
    )
    grad_bvalue = jnp.sum(grad_value.astype(jnp.float32), axis=0).T
    in_part = jnp.einsum("she,ehd->sd", grad_query, query_w, preferred_element_type=jnp.float32)
    in_part = in_part + jnp.einsum(
        "she,ehd->sd", grad_key, key_w, preferred_element_type=jnp.float32
    )
    in_part = in_part + jnp.einsum(
        "she,ehd->sd", grad_value, value_w, preferred_element_type=jnp.float32
    )
    grad_normed_in = lax.psum(in_part.astype(jnp.bfloat16), "tensor").astype(jnp.float32)
    unused_in, pull_in = jax.vjp(normed, tok_float, gain_in)
    grad_in_norm, grad_gattn = pull_in(grad_normed_in)
    grad_tokens = grad_middle + grad_in_norm
    every_sum = (
        lax.psum_scatter(grad_gattn, "dp", scatter_dimension=0, tiled=True),
        lax.psum_scatter(grad_wquery, "dp", scatter_dimension=0, tiled=True),
        lax.psum_scatter(grad_bquery, "dp", scatter_dimension=0, tiled=True),
        lax.psum_scatter(grad_wkey, "dp", scatter_dimension=0, tiled=True),
        lax.psum_scatter(grad_wvalue, "dp", scatter_dimension=0, tiled=True),
        lax.psum_scatter(grad_bvalue, "dp", scatter_dimension=0, tiled=True),
        lax.psum_scatter(grad_wout, "dp", scatter_dimension=0, tiled=True),
        lax.psum_scatter(grad_gmlp, "dp", scatter_dimension=0, tiled=True),
        lax.psum_scatter(grad_wgate, "dp", scatter_dimension=0, tiled=True),
        lax.psum_scatter(grad_wup, "dp", scatter_dimension=0, tiled=True),
        lax.psum_scatter(grad_wdown, "dp", scatter_dimension=0, tiled=True),
    )
    attn_grads = every_sum[:7]
    mlp_grads = every_sum[7:]
    return (
        out_tokens,
        grad_tokens,
        attn_grads[0],
        attn_grads[1],
        attn_grads[2],
        attn_grads[3],
        key_bias_total,
        attn_grads[4],
        attn_grads[5],
        attn_grads[6],
        mlp_grads[0],
        mlp_grads[1],
        mlp_grads[2],
        mlp_grads[3],
    )


MESH = pl.DeviceIdType.MESH
BF = jnp.bfloat16
F32 = jnp.float32
NT = (((1,), (1,)), ((), ()))
NN = (((1,), (0,)), ((), ()))
TN = (((0,), (0,)), ((), ()))
VMEM_LIMIT = 62 * 2**20
ANY = pl.BlockSpec(memory_space=pl.ANY)
VM = pl.BlockSpec(memory_space=pltpu.VMEM)


def dot(a, b, dims):
    return lax.dot_general(a, b, dims, preferred_element_type=F32)


class Spot:
    def __init__(self, nz):
        self.nz = nz
        self.dp = lax.axis_index("dp")
        self.t = lax.axis_index("tensor")
        self.z, self.x, self.c = self.dp // 4, (self.dp // 2) % 2, self.dp % 2
        self.xn = (self.index(self.z, 1 - self.x, self.c), self.t)
        self.cn = (self.index(self.z, self.x, 1 - self.c), self.t)
        self.yn = (self.dp, 1 - self.t)

    def index(self, z, x, c):
        return (z * 2 + x) * 2 + c

    def near(self, k):
        nz, z = self.nz, self.z
        edge = jnp.minimum(z, nz - 1 - z)
        side = jnp.where(z <= nz - 1 - z, -1, 1)
        half = (k + 1) // 2
        close = side * half if k % 2 else -side * half
        return z + jnp.where(k <= 2 * edge, close, -side * (k - edge))

    def zn(self, k):
        return (self.index(self.near(k), self.x, self.c), self.t)


class Wires:
    def __init__(self):
        self.sent = []

    def send(self, src, dst, send_sem, recv_sem, device):
        copy = pltpu.make_async_remote_copy(
            src_ref=src,
            dst_ref=dst,
            send_sem=send_sem,
            recv_sem=recv_sem,
            device_id=device,
            device_id_type=MESH,
        )
        copy.start()
        self.sent.append(copy)

    def landed(self, dst, recv_sem, spot):
        pltpu.make_async_remote_copy(
            src_ref=dst,
            dst_ref=dst,
            send_sem=recv_sem,
            recv_sem=recv_sem,
            device_id=spot.xn,
            device_id_type=MESH,
        ).wait_recv()

    def drain(self):
        for copy in self.sent:
            copy.wait_send()
        self.sent = []


def greet(devices):
    barrier = pltpu.get_barrier_semaphore()
    for device in devices:
        pl.semaphore_signal(barrier, inc=1, device_id=device, device_id_type=MESH)
    pl.semaphore_wait(barrier, len(devices))


def gather_kernel(
    nz,
    qkv_in,
    wo_in,
    small_in,
    cot_in,
    gate_in,
    up_in,
    down_in,
    qkv,
    wo,
    small,
    cot,
    mlp_w,
    stage_a,
    stage_b,
    stage_c,
    local_sem,
    a_recv,
    a_send,
    s_recv,
    s_send,
    c_recv,
    c_send,
    w_recv,
    w_send,
):
    at = Spot(nz)
    ndp = 4 * nz
    half = cot_in.shape[0] // 2
    rows = qkv_in.shape[1]
    others = [(lax.rem(at.dp + p, ndp), at.t) for p in range(1, ndp)]
    greet(others + [at.yn])
    wires = Wires()

    def part(ref, owner):
        return ref.at[:, pl.ds(pl.multiple_of(owner * rows, rows), rows), :]

    def send_attn(own, owner, slot, device):
        for i, (src, dst) in enumerate(((qkv_in, qkv), (wo_in, wo))):
            to = part(dst, owner)
            wires.send(src if own else to, to, a_send.at[i, slot], a_recv.at[i, owner], device)

    def wait_attn(owner):
        for i, dst in enumerate((qkv, wo)):
            wires.landed(part(dst, owner), a_recv.at[i, owner], at)

    slot = 0
    send_attn(True, at.dp, 0, at.xn)
    send_attn(True, at.dp, 1, at.cn)
    for k in range(1, nz):
        send_attn(True, at.dp, 1 + k, at.zn(k))
    mine = at.c * 2 + at.t
    for i, src in enumerate((gate_in, up_in, down_in)):
        wires.send(src, mlp_w.at[i, mine], w_send.at[0, i], w_recv.at[i, mine], at.yn)
        wires.send(src, mlp_w.at[i, mine], w_send.at[1, i], w_recv.at[i, mine], at.cn)
    for p, device in enumerate(others):
        wires.send(small_in, small.at[at.dp], s_send.at[p], s_recv.at[at.dp], device)
    cot_own = cot_in.at[pl.ds(pl.multiple_of(at.t * half, half), half), :]
    for k in range(1, nz):
        wires.send(cot_own, cot.at[at.z, at.x], c_send.at[k], c_recv.at[at.z, at.x], at.zn(k))
    loads = [
        pltpu.make_async_copy(qkv_in, stage_a, local_sem.at[0]),
        pltpu.make_async_copy(wo_in, stage_b, local_sem.at[1]),
        pltpu.make_async_copy(small_in, stage_c, local_sem.at[2]),
    ]
    stores = [
        pltpu.make_async_copy(stage_a, part(qkv, at.dp), local_sem.at[3]),
        pltpu.make_async_copy(stage_b, part(wo, at.dp), local_sem.at[4]),
        pltpu.make_async_copy(stage_c, small.at[at.dp], local_sem.at[5]),
    ]
    for load in loads:
        load.start()
    for load, store in zip(loads, stores):
        load.wait()
        store.start()
    for k in range(nz):
        if k:
            owner = at.index(at.near(k), at.x, at.c)
            wait_attn(owner)
            send_attn(False, owner, nz + 2 * k, at.xn)
            send_attn(False, owner, nz + 2 * k + 1, at.cn)
        owner = at.index(at.near(k), 1 - at.x, at.c)
        wait_attn(owner)
        send_attn(False, owner, 3 * nz + k, at.cn)
    wires.send(cot_own, cot.at[at.z, at.x], c_send.at[0], c_recv.at[at.z, at.x], at.xn)
    for k in range(nz):
        zk = at.near(k)
        if k:
            wires.landed(cot.at[zk, at.x], c_recv.at[zk, at.x], at)
            wires.send(cot.at[zk, at.x], cot.at[zk, at.x], c_send.at[nz + k], c_recv.at[zk, at.x], at.xn)
        wires.landed(cot.at[zk, 1 - at.x], c_recv.at[zk, 1 - at.x], at)
    across = at.c * 2 + 1 - at.t
    for i in range(3):
        wires.landed(mlp_w.at[i, across], w_recv.at[i, across], at)
        wires.send(mlp_w.at[i, across], mlp_w.at[i, across], w_send.at[2, i], w_recv.at[i, across], at.cn)
    for i in range(3):
        for tt in range(2):
            there = (1 - at.c) * 2 + tt
            wires.landed(mlp_w.at[i, there], w_recv.at[i, there], at)
    for device in others:
        wires.landed(small.at[device[0]], s_recv.at[device[0]], at)
    for zz in range(nz):
        for xx in range(2):
            wait_attn(at.index(zz, xx, 1 - at.c))
    for store in stores:
        store.wait()
    wires.drain()


def gather_weights(nz, qkv, wo, small, cotangent, gate, up, down):
    ndp = 4 * nz
    half, wide = cotangent.shape[0] // 2, cotangent.shape[1]
    shape = jax.ShapeDtypeStruct
    dma = pltpu.SemaphoreType.DMA
    return pl.pallas_call(
        functools.partial(gather_kernel, nz),
        out_shape=(
            shape((qkv.shape[0], ndp * qkv.shape[1], wide), BF),
            shape((wo.shape[0], ndp * wo.shape[1], wide), BF),
            shape((ndp,) + small.shape, BF),
            shape((nz, 2, half, wide), BF),
            shape((3, 4) + gate.shape, BF),
        ),
        in_specs=[ANY] * 7,
        out_specs=[ANY] * 5,
        scratch_shapes=[
            pltpu.VMEM(qkv.shape, BF),
            pltpu.VMEM(wo.shape, BF),
            pltpu.VMEM(small.shape, BF),
            dma((6,)),
            dma((2, ndp)),
            dma((2, 4 * nz)),
            dma((ndp,)),
            dma((ndp,)),
            dma((nz, 2)),
            dma((2 * nz,)),
            dma((3, 4)),
            dma((3, 3)),
        ],
        compiler_params=pltpu.CompilerParams(
            collective_id=1, has_side_effects=True, vmem_limit_bytes=VMEM_LIMIT
        ),
        name="gather_weights",
    )(qkv, wo, small, cotangent, gate, up, down)


def mlp_kernel(
    nz,
    tok_in,
    part_in,
    gain_in,
    cot_in,
    mlp_in,
    cot_own_in,
    gate_in,
    up_in,
    down_in,
    out_part,
    grads,
    mid_low,
    mid_half,
    grad_gain,
    weights,
    cot,
    nm,
    gh,
    hid,
    gg,
    gu,
    own,
    xs,
    xr,
    zs,
    zr,
    pair,
    ysend,
    yrecv,
    gain_recv,
    gain_send,
    wide_acc,
    local_sem,
    n_recv,
    n_send,
    x_recv,
    x_send,
    z_recv,
    z_send,
    y_recv,
    y_send,
):
    at = Spot(nz)
    half, wide = nm.shape[2], nm.shape[3]
    two = 2 * half
    shard = mlp_in.shape[2]
    padded = weights.shape[2]
    units = 4 * padded
    wires = Wires()
    mine = at.c * 2 + at.t

    loads = []

    def load(src, dst, sem):
        copy = pltpu.make_async_copy(src, dst, sem)
        copy.start()
        loads.append(copy)
        return copy

    per = [[], [], []]
    for i, src in ((2, down_in), (0, gate_in), (1, up_in)):
        per[i].append(load(src, weights.at[i, mine, pl.ds(0, shard)], local_sem.at[i * 4]))
        for j, slot in enumerate((at.c * 2 + 1 - at.t, (1 - at.c) * 2, (1 - at.c) * 2 + 1)):
            per[i].append(
                load(mlp_in.at[i, slot], weights.at[i, slot, pl.ds(0, shard)], local_sem.at[i * 4 + 1 + j])
            )
    cot_loads = [
        load(
            cot_own_in.at[pl.ds(pl.multiple_of(at.t * half, half), half), :],
            cot.at[at.z, at.x],
            local_sem.at[12],
        )
    ]
    for k in range(nz):
        zk = at.near(k)
        if k:
            cot_loads.append(load(cot_in.at[zk, at.x], cot.at[zk, at.x], local_sem.at[12 + 2 * k]))
        cot_loads.append(load(cot_in.at[zk, 1 - at.x], cot.at[zk, 1 - at.x], local_sem.at[13 + 2 * k]))
    for i in range(3):
        for s in range(4):
            weights[i, s, shard:padded, :] = jnp.zeros((padded - shard, wide), BF)

    far_row = pl.multiple_of((1 - at.t) * half, half)
    own_row = pl.multiple_of(at.t * half, half)
    greet([at.xn, at.yn] + [at.zn(k) for k in range(1, nz)])
    ysend[0] = part_in[pl.ds(far_row, half), :].astype(BF)
    wires.send(ysend.at[0], yrecv.at[0], y_send.at[0], y_recv.at[0], at.yn)
    for copy in per[2] + cot_loads:
        copy.wait()
    down_w = weights.at[2]

    for k in range(nz):
        zk = at.near(k)
        gh[zk] = dot(cot[zk].reshape(two, wide), down_w[...].reshape(units, wide), NT)

    wires.landed(yrecv.at[0], y_recv.at[0], at)
    middle = (
        tok_in[pl.ds(own_row, half), :].astype(F32)
        + part_in[pl.ds(own_row, half), :]
        + yrecv[0].astype(F32)
    )
    gain = gain_in[...]
    rms = lax.rsqrt(jnp.mean(middle * middle, axis=-1, keepdims=True) + EPS)
    mid_half[...] = middle
    nm[at.z, at.x] = (middle * rms * gain).astype(BF)

    mine_nm = nm.at[at.z, at.x]
    wires.send(mine_nm, mine_nm, n_send.at[0], n_recv.at[at.z, at.x], at.xn)
    for k in range(1, nz):
        wires.send(mine_nm, mine_nm, n_send.at[k], n_recv.at[at.z, at.x], at.zn(k))
    for copy in per[0] + per[1]:
        copy.wait()
    gate_w, up_w = weights.at[0], weights.at[1]

    def column_sum(k):
        zk = at.near(k)
        wires.landed(xr.at[k], x_recv.at[k], at)
        total = own[k] + xr[k].astype(F32)
        if k == 0:
            own[0] = total
        else:
            zs[k] = total.astype(BF)
            wires.send(zs.at[k], zr.at[at.z], z_send.at[k], z_recv.at[at.z], at.zn(k))

    for k in range(nz):
        zk = at.near(k)
        if k:
            ref = nm.at[zk, at.x]
            wires.landed(ref, n_recv.at[zk, at.x], at)
            wires.send(ref, ref, n_send.at[nz + k], n_recv.at[zk, at.x], at.xn)
        ref = nm.at[zk, 1 - at.x]
        wires.landed(ref, n_recv.at[zk, 1 - at.x], at)
        a = nm[zk].reshape(two, wide)
        gate = dot(a, gate_w[...].reshape(units, wide), NT)
        up = dot(a, up_w[...].reshape(units, wide), NT)
        sig = jax.nn.sigmoid(gate)
        silu = gate * sig
        hid[zk] = (silu * up).astype(BF)
        ghk = gh[zk]
        gg[zk] = (ghk * up * sig * (1.0 + gate * (1.0 - sig))).astype(BF)
        gu[zk] = (ghk * silu).astype(BF)
        pair[...] = (
            dot(gg[zk], gate_w[...].reshape(units, wide), NN)
            + dot(gu[zk], up_w[...].reshape(units, wide), NN)
        ).reshape(2, half, wide)
        xs[k] = pair[1 - at.x].astype(BF)
        wires.send(xs.at[k], xr.at[k], x_send.at[k], x_recv.at[k], at.xn)
        own[k] = pair[at.x]
        if k:
            column_sum(k - 1)

    for k in range(nz):
        zk = at.near(k)
        out_part[zk] = dot(hid[zk], down_w[...].reshape(units, wide), NN).astype(BF).reshape(2, half, wide)
    column_sum(nz - 1)

    tile = 512
    for i, (lhs, rhs) in enumerate(((gg, nm), (gu, nm), (hid, cot))):
        left = lhs[...].reshape(nz * two, units)
        for j in range(wide // tile):
            cols = slice(j * tile, (j + 1) * tile)
            right = rhs[:, :, :, cols].reshape(nz * two, tile)
            acc = dot(left, right, TN).astype(BF).reshape(4, padded, tile)
            grads[i, :, :, cols] = acc[:, :shard]

    total = own[0]
    for k in range(1, nz):
        zk = at.near(k)
        wires.landed(zr.at[zk], z_recv.at[zk], at)
        total = total + zr[zk].astype(F32)
    middle = mid_half[...]
    rms = lax.rsqrt(jnp.mean(middle * middle, axis=-1, keepdims=True) + EPS)
    unit = middle * rms
    gain_send[...] = jnp.sum(total * unit, axis=0, keepdims=True)
    scaled = total * gain
    cot_f = cot[at.z, at.x].astype(F32)
    grad_mid = cot_f + rms * (scaled - unit * jnp.mean(scaled * unit, axis=-1, keepdims=True))
    ysend[1] = grad_mid.astype(BF)
    wires.send(ysend.at[1], yrecv.at[1], y_send.at[1], y_recv.at[1], at.yn)
    wires.send(gain_send, gain_recv, y_send.at[2], y_recv.at[2], at.yn)
    mid_low[at.t] = ysend[1]
    wires.landed(yrecv.at[1], y_recv.at[1], at)
    wires.landed(gain_recv, y_recv.at[2], at)
    mid_low[1 - at.t] = yrecv[1]
    grad_gain[...] = gain_send[...] + gain_recv[...]
    wires.drain()


def mlp_step(nz, tokens, part, gain, cot_all, mlp_all, cotangent, gate, up, down):
    half, wide = cotangent.shape[0] // 2, cotangent.shape[1]
    shard = gate.shape[0]
    padded = -(-shard // 32) * 32
    units = 4 * padded
    shape = jax.ShapeDtypeStruct
    dma = pltpu.SemaphoreType.DMA
    vm = pltpu.VMEM
    return pl.pallas_call(
        functools.partial(mlp_kernel, nz),
        out_shape=(
            shape((nz, 2, half, wide), BF),
            shape((3, 4, shard, wide), BF),
            shape((2, half, wide), BF),
            shape((half, wide), F32),
            shape((1, wide), F32),
        ),
        in_specs=[VM, VM, VM] + [ANY] * 6,
        out_specs=[VM] * 5,
        scratch_shapes=[
            vm((3, 4, padded, wide), BF),
            vm((nz, 2, half, wide), BF),
            vm((nz, 2, half, wide), BF),
            vm((nz, 2 * half, units), F32),
            vm((nz, 2 * half, units), BF),
            vm((nz, 2 * half, units), BF),
            vm((nz, 2 * half, units), BF),
            vm((nz, half, wide), F32),
            vm((nz, half, wide), BF),
            vm((nz, half, wide), BF),
            vm((nz, half, wide), BF),
            vm((nz, half, wide), BF),
            vm((2, half, wide), F32),
            vm((2, half, wide), BF),
            vm((2, half, wide), BF),
            vm((1, wide), F32),
            vm((1, wide), F32),
            vm((8, 128), F32),
            dma((12 + 2 * nz + 2,)),
            dma((nz, 2)),
            dma((2 * nz,)),
            dma((nz,)),
            dma((nz,)),
            dma((nz,)),
            dma((nz,)),
            dma((3,)),
            dma((3,)),
        ],
        compiler_params=pltpu.CompilerParams(
            collective_id=2, has_side_effects=True, vmem_limit_bytes=VMEM_LIMIT
        ),
        name="mlp_step",
    )(tokens, part, gain, cot_all, mlp_all, cotangent, gate, up, down)


def tail_kernel(
    nz,
    gq_in,
    go_in,
    out_part,
    mid_half,
    in_part,
    tok_in,
    mid_low,
    gain_in,
    gmlp_in,
    bias_in,
    gq,
    go,
    out_tokens,
    grad_tokens,
    small,
    q_core,
    o_core,
    q_send,
    o_send,
    q_x,
    o_x,
    q_zs,
    o_zs,
    q_z,
    o_z,
    b_x,
    b_zs,
    b_z,
    osend,
    orecv,
    irecv,
    a_recv,
    a_send,
    x_recv,
    x_send,
    z_recv,
    z_send,
    b_xrecv,
    b_xsend,
    b_zrecv,
    b_zsend,
    y_recv,
    y_send,
    s_recv,
    s_send,
    small_all,
):
    at = Spot(nz)
    ndp = 4 * nz
    half = mid_half.shape[0]
    others = [(lax.rem(at.dp + p, ndp), at.t) for p in range(1, ndp)]
    greet(others + [at.yn])
    wires = Wires()
    mats = ((gq_in, q_core, q_send, q_x, q_zs, q_z), (go_in, o_core, o_send, o_x, o_zs, o_z))
    wires.send(in_part, irecv, y_send.at[0], y_recv.at[0], at.yn)
    for k in range(nz):
        zk = at.near(k)
        for xx in (1, 0):
            xk = 1 - at.x if xx else at.x
            for i, (src, core, _, _, _, _) in enumerate(mats):
                wires.send(
                    src.at[at.index(zk, xk, 1 - at.c)],
                    core.at[k, xx],
                    a_send.at[i, k, xx],
                    a_recv.at[i, k, xx],
                    at.cn,
                )
    for k in range(nz):
        zk = at.near(k)
        for i, (src, core, send, xbuf, _, _) in enumerate(mats):
            wires.landed(core.at[k, 1], a_recv.at[i, k, 1], at)
            mine = src[at.index(zk, 1 - at.x, at.c)].astype(F32) + core[k, 1].astype(F32)
            send[k] = mine.astype(BF)
            wires.send(send.at[k], xbuf.at[k], x_send.at[i, k], x_recv.at[i, k], at.xn)
    for k in range(nz):
        zk = at.near(k)
        wires.send(out_part.at[zk, 1 - at.x], b_x.at[k], b_xsend.at[k], b_xrecv.at[k], at.xn)
    for k in list(range(1, nz)) + [0]:
        zk = at.near(k)
        for i, (src, core, _, xbuf, zsend, zbuf) in enumerate(mats):
            wires.landed(core.at[k, 0], a_recv.at[i, k, 0], at)
            wires.landed(xbuf.at[k], x_recv.at[i, k], at)
            total = (
                src[at.index(zk, at.x, at.c)].astype(F32)
                + core[k, 0].astype(F32)
                + xbuf[k].astype(F32)
            )
            if k:
                zsend[k] = total.astype(BF)
                wires.send(zsend.at[k], zbuf.at[at.z], z_send.at[i, k], z_recv.at[i, at.z], at.zn(k))
            else:
                (gq, go)[i][...] = total
    wires.landed(irecv, y_recv.at[0], at)
    grad_in = in_part[...].astype(F32) + irecv[...].astype(F32)
    tok = tok_in[...].astype(F32)
    rms = lax.rsqrt(jnp.mean(tok * tok, axis=-1, keepdims=True) + EPS)
    unit = tok * rms
    grad_gain = jnp.sum(grad_in * unit, axis=0, keepdims=True)
    scaled = grad_in * gain_in[...]
    grad_tokens[...] = mid_low[...].astype(F32) + rms * (
        scaled - unit * jnp.mean(scaled * unit, axis=-1, keepdims=True)
    )
    lanes = small.shape[1]
    steps = grad_gain.shape[1] // lanes
    gmlp = gmlp_in[...]
    for i in range(steps):
        small_all[at.dp, i : i + 1, :] = grad_gain[:, i * lanes : (i + 1) * lanes]
        small_all[at.dp, steps + i : steps + i + 1, :] = gmlp[:, i * lanes : (i + 1) * lanes]
    small_all[at.dp, 2 * steps :, :] = bias_in[...]
    for p, device in enumerate(others):
        wires.send(small_all.at[at.dp], small_all.at[at.dp], s_send.at[p], s_recv.at[at.dp], device)
    for k in list(range(1, nz)) + [0]:
        zk = at.near(k)
        wires.landed(b_x.at[k], b_xrecv.at[k], at)
        total = out_part[zk, at.x].astype(F32) + b_x[k].astype(F32)
        if k:
            b_zs[k] = total.astype(BF)
            wires.send(b_zs.at[k], b_z.at[at.z], b_zsend.at[k], b_zrecv.at[at.z], at.zn(k))
        else:
            out_total = total + mid_half[...]
    for k in range(1, nz):
        zk = at.near(k)
        for i, buf in enumerate((q_z, o_z)):
            wires.landed(buf.at[zk], z_recv.at[i, zk], at)
            ref = (gq, go)[i]
            ref[...] += buf[zk].astype(F32)
    for k in range(1, nz):
        zk = at.near(k)
        wires.landed(b_z.at[zk], b_zrecv.at[zk], at)
        out_total = out_total + b_z[zk].astype(F32)
    osend[...] = out_total.astype(BF)
    wires.send(osend, orecv, y_send.at[1], y_recv.at[1], at.yn)
    out_tokens[at.t] = osend[...]
    for device in others:
        wires.landed(small_all.at[device[0]], s_recv.at[device[0]], at)
    total = small_all[0]
    for p in range(1, ndp):
        total = total + small_all[p]
    small[...] = total
    wires.landed(orecv, y_recv.at[1], at)
    out_tokens[1 - at.t] = orecv[...]
    wires.drain()


def tail_step(nz, gq, go, out_part, mid_half, in_part, tokens, mid_low, gain, gmlp, bias):
    ndp = 4 * nz
    half, wide = mid_half.shape
    shape = jax.ShapeDtypeStruct
    dma = pltpu.SemaphoreType.DMA
    vm = pltpu.VMEM
    qb, ob = gq.shape[1:], go.shape[1:]
    lanes = bias.shape[1]
    srows = 2 * (wide // lanes) + bias.shape[0]
    return pl.pallas_call(
        functools.partial(tail_kernel, nz),
        out_shape=(
            shape(qb, F32),
            shape(ob, F32),
            shape((2, half, wide), BF),
            shape((2 * half, wide), F32),
            shape((srows, lanes), F32),
        ),
        in_specs=[VM] * 10,
        out_specs=[VM] * 5,
        scratch_shapes=[
            vm((nz, 2) + qb, BF),
            vm((nz, 2) + ob, BF),
            vm((nz,) + qb, BF),
            vm((nz,) + ob, BF),
            vm((nz,) + qb, BF),
            vm((nz,) + ob, BF),
            vm((nz,) + qb, BF),
            vm((nz,) + ob, BF),
            vm((nz,) + qb, BF),
            vm((nz,) + ob, BF),
            vm((nz, half, wide), BF),
            vm((nz, half, wide), BF),
            vm((nz, half, wide), BF),
            vm((half, wide), BF),
            vm((half, wide), BF),
            vm((2 * half, wide), BF),
            dma((2, nz, 2)),
            dma((2, nz, 2)),
            dma((2, nz)),
            dma((2, nz)),
            dma((2, nz)),
            dma((2, nz)),
            dma((nz,)),
            dma((nz,)),
            dma((nz,)),
            dma((nz,)),
            dma((2,)),
            dma((2,)),
            dma((ndp,)),
            dma((ndp,)),
            vm((ndp, srows, lanes), F32),
        ],
        compiler_params=pltpu.CompilerParams(
            collective_id=3, has_side_effects=True, vmem_limit_bytes=VMEM_LIMIT
        ),
        name="tail_step",
    )(gq, go, out_part, mid_half, in_part, tokens, mid_low, gain, gmlp, bias)


def rotate_heads(field, flip_sign):
    half_dim = field.shape[-1] // 2
    places = jnp.arange(field.shape[1], dtype=F32)
    freqs = ROPE_BASE ** (-(jnp.arange(half_dim, dtype=F32) * 2.0 / field.shape[-1]))
    angles = places[:, None] * freqs[None, :]
    cosine = jnp.cos(angles)[None]
    sine = flip_sign * jnp.sin(angles)[None]
    first = field[..., :half_dim]
    second = field[..., half_dim:]
    return jnp.concatenate(
        [first * cosine - second * sine, second * cosine + first * sine], axis=-1
    )


def core_swap(ndp):
    return [(d, d + 1 - 2 * (d % 2)) for d in range(ndp)]


def planes(
    tokens,
    prefix,
    g_attn,
    w_query,
    b_query,
    w_key,
    b_key,
    w_value,
    b_value,
    w_out,
    g_mlp,
    w_gate,
    w_up,
    w_down,
    cotangent,
    ndp,
):
    nz = ndp // 4
    seq_len, wide = tokens.shape
    rows, heads = b_query.shape
    head_dim = rows * ndp
    dp = lax.axis_index("dp")
    t = lax.axis_index("tensor")
    gshare = g_attn.shape[0]

    def heads_first(w):
        return jnp.swapaxes(w, 0, 1)

    qkv_own = jnp.concatenate([heads_first(w_query), heads_first(w_key), heads_first(w_value)], axis=0)
    wo_own = heads_first(w_out)

    def row(v):
        flat = v.reshape(1, -1)
        return jnp.pad(flat, ((0, 0), (0, 128 - flat.shape[1])))

    small_own = jnp.concatenate(
        [row(g_attn), row(g_mlp), row(b_query.T), row(b_value)] + [jnp.zeros((4, 128), BF)], axis=0
    )
    qkv_w, out_w, small, cot_all, mlp_all = gather_weights(
        nz, qkv_own, wo_own, small_own, cotangent, w_gate, w_up, w_down
    )
    gain_in = small[:, 0, :gshare].reshape(1, wide).astype(F32)
    gain_mid = small[:, 1, :gshare].reshape(1, wide).astype(F32)
    query_b = small[:, 2, : heads * rows].reshape(ndp, heads, rows).transpose(1, 0, 2).reshape(heads, 1, head_dim)
    value_b = small[:, 3, :rows].reshape(1, 1, head_dim)
    key_b = b_key.T.reshape(1, 1, head_dim)
    bias = jnp.concatenate([query_b, key_b, value_b], axis=0).astype(F32)

    tok_float = tokens.astype(F32)
    normed_in = normed(tok_float, gain_in).astype(BF)
    pre = jnp.einsum("sd,ked->kse", normed_in, qkv_w, preferred_element_type=F32) + bias
    score_scale = head_dim ** (-0.5)
    rot = rotate_heads(pre[: heads + 1], 1.0).astype(BF)
    query_rot, key_rot = rot[:heads], rot[heads]
    value_low = pre[heads + 1].astype(BF)
    row_index = lax.broadcasted_iota(jnp.int32, (seq_len, seq_len), 0)
    col_index = lax.broadcasted_iota(jnp.int32, (seq_len, seq_len), 1)
    allowed = (col_index <= row_index) | (col_index < prefix[0])
    raw_scores = jnp.einsum("gsd,td->gst", query_rot, key_rot, preferred_element_type=F32) * score_scale
    scores = jnp.where(allowed, raw_scores, NEG_BIG)
    row_peak = jnp.max(scores, axis=-1, keepdims=True)
    shifted_exp = jnp.exp(scores - row_peak)
    row_total = jnp.sum(shifted_exp, axis=-1, keepdims=True)
    probs = shifted_exp / row_total
    probs_low = probs.astype(BF)
    attended = jnp.einsum("gst,td->gsd", probs_low, value_low, preferred_element_type=F32)
    attended_low = attended.astype(BF)
    attn_part = jnp.einsum("gse,ged->sd", attended_low, out_w, preferred_element_type=F32)

    out_part, grads, mid_low, mid_half, gmlp = mlp_step(
        nz, tokens, attn_part, gain_mid, cot_all, mlp_all, cotangent, w_gate, w_up, w_down
    )

    core = dp % 2
    keep = lax.dynamic_slice_in_dim(grads, core * 2, 2, axis=1)
    give = lax.dynamic_slice_in_dim(grads, (1 - core) * 2, 2, axis=1)
    got = lax.ppermute(give, "dp", core_swap(ndp))
    chip = keep.astype(F32) + got.astype(F32)
    chip_own = lax.dynamic_slice_in_dim(chip, t, 1, axis=1)[:, 0]
    chip_give = lax.dynamic_slice_in_dim(chip, 1 - t, 1, axis=1)[:, 0].astype(BF)
    chip_got = lax.ppermute(chip_give, "tensor", [(0, 1), (1, 0)])
    mlp_grads = chip_own + chip_got.astype(F32)

    middle_low = mid_low.reshape(seq_len, wide)
    grad_wout = jnp.einsum("gse,sd->ged", attended_low, middle_low, preferred_element_type=F32).astype(BF)
    grad_attended = jnp.einsum("sd,ged->gse", middle_low, out_w, preferred_element_type=F32).astype(BF)
    grad_value = jnp.einsum("gst,gsd->td", probs_low, grad_attended, preferred_element_type=F32).astype(BF)
    grad_probs = jnp.einsum("gsd,td->gst", grad_attended, value_low, preferred_element_type=F32)
    inner_sum = jnp.sum(probs * grad_probs, axis=-1, keepdims=True)
    grad_scores = (probs * (grad_probs - inner_sum)).astype(BF)
    grad_qrot = jnp.einsum("gst,td->gsd", grad_scores, key_rot, preferred_element_type=F32) * score_scale
    grad_krot = jnp.einsum("gst,gsd->td", grad_scores, query_rot, preferred_element_type=F32) * score_scale
    back = rotate_heads(jnp.concatenate([grad_qrot, grad_krot[None]], axis=0), -1.0).astype(BF)
    grad_pre = jnp.concatenate([back, grad_value[None]], axis=0)
    grad_w = jnp.einsum("kse,sd->ked", grad_pre, normed_in, preferred_element_type=F32).astype(BF)
    grad_b = jnp.sum(grad_pre.astype(F32), axis=1)
    in_part = jnp.einsum("kse,ked->sd", grad_pre, qkv_w, preferred_element_type=F32).astype(BF)

    def by_owner(g):
        return g.reshape(g.shape[0], ndp, rows, wide).transpose(1, 0, 2, 3).reshape(ndp, -1, wide)

    lanes = wide // 3
    gq, go, out_tokens, grad_tokens, sums = tail_step(
        nz,
        by_owner(grad_w),
        by_owner(grad_wout),
        out_part,
        mid_half,
        in_part,
        tokens,
        middle_low,
        gain_in,
        gmlp,
        grad_b.reshape(-1, lanes),
    )
    gq = gq.reshape(heads + 2, rows, wide).transpose(1, 0, 2)
    go = go.reshape(heads, rows, wide).transpose(1, 0, 2)
    gattn_all = sums[:3].reshape(wide)
    gmlp_all = sums[3:6].reshape(wide)
    bias_all = sums[6:].reshape(heads + 2, head_dim).T
    bias_own = lax.dynamic_slice_in_dim(bias_all, dp * rows, rows, axis=0)
    return (
        out_tokens.reshape(seq_len, wide),
        grad_tokens,
        lax.dynamic_slice_in_dim(gattn_all, dp * gshare, gshare),
        gq[:, :heads],
        bias_own[:, :heads],
        gq[:, heads : heads + 1],
        bias_all[:, heads : heads + 1],
        gq[:, heads + 1 :],
        bias_own[:, heads + 1 :],
        go,
        lax.dynamic_slice_in_dim(gmlp_all, dp * gshare, gshare),
        mlp_grads[0],
        mlp_grads[1],
        mlp_grads[2],
    )


def local(*arrays, ndp):
    rows, heads = arrays[4].shape
    shard = arrays[11].shape[0]
    if ndp % 4 == 0 and rows % 8 == 0 and shard % 8 == 0 and heads * rows <= 128:
        return planes(*arrays, ndp=ndp)
    return whole_gather(*arrays)


def solution(mesh):
    in_specs = (
        P("dp", None),
        P("dp"),
        P("dp"),
        P("dp", "tensor", None),
        P("dp", "tensor"),
        P("dp", "tensor", None),
        P(None, "tensor"),
        P("dp", "tensor", None),
        P("dp", "tensor"),
        P("dp", "tensor", None),
        P("dp"),
        P(("dp", "tensor"), None),
        P(("dp", "tensor"), None),
        P(("dp", "tensor"), None),
        P("dp", None),
    )
    out_specs = (
        P("dp", None),
        P("dp", None),
        P("dp"),
        P("dp", "tensor", None),
        P("dp", "tensor"),
        P("dp", "tensor", None),
        P(None, "tensor"),
        P("dp", "tensor", None),
        P("dp", "tensor"),
        P("dp", "tensor", None),
        P("dp"),
        P(("dp", "tensor"), None),
        P(("dp", "tensor"), None),
        P(("dp", "tensor"), None),
    )
    return jax.shard_map(functools.partial(local, ndp=mesh.shape["dp"]), mesh=mesh, in_specs=in_specs, out_specs=out_specs, check_vma=False)
```

```python
import functools

import jax
import jax.numpy as jnp
import numpy as np
from jax import lax
from jax.experimental import pallas as pl
from jax.experimental.pallas import tpu as pltpu
from jax.sharding import PartitionSpec as P

EPS = 1e-06
ROPE_BASE = 1000000.0
NEG_BIG = -1e30


def rotate(field, flip_sign):
    half_dim = field.shape[-1] // 2
    places = jnp.arange(field.shape[0], dtype=jnp.float32)
    freqs = ROPE_BASE ** (-(jnp.arange(half_dim, dtype=jnp.float32) * 2.0 / field.shape[-1]))
    angles = places[:, None] * freqs[None, :]
    cosine = jnp.cos(angles)[:, None, :]
    sine = flip_sign * jnp.sin(angles)[:, None, :]
    first = field[..., :half_dim]
    second = field[..., half_dim:]
    return jnp.concatenate(
        [first * cosine - second * sine, second * cosine + first * sine], axis=-1
    )


def normed(field, gain):
    return field * lax.rsqrt(jnp.mean(field * field, axis=-1, keepdims=True) + EPS) * gain


def whole_gather(
    tokens,
    prefix,
    g_attn,
    w_query,
    b_query,
    w_key,
    b_key,
    w_value,
    b_value,
    w_out,
    g_mlp,
    w_gate,
    w_up,
    w_down,
    cotangent,
):
    gain_one, query_w, query_b, key_w, value_w, value_b, out_w = (
        lax.all_gather(g_attn, "dp", axis=0, tiled=True),
        lax.all_gather(w_query, "dp", axis=0, tiled=True),
        lax.all_gather(b_query, "dp", axis=0, tiled=True),
        lax.all_gather(w_key, "dp", axis=0, tiled=True),
        lax.all_gather(w_value, "dp", axis=0, tiled=True),
        lax.all_gather(b_value, "dp", axis=0, tiled=True),
        lax.all_gather(w_out, "dp", axis=0, tiled=True),
    )
    tok_float = tokens.astype(jnp.float32)
    gain_in = gain_one.astype(jnp.float32)
    normed_in = normed(tok_float, gain_in).astype(jnp.bfloat16)
    query_pre = (
        jnp.einsum("sd,ehd->she", normed_in, query_w, preferred_element_type=jnp.float32)
        + query_b.astype(jnp.float32).T
    )
    key_pre = (
        jnp.einsum("sd,ehd->she", normed_in, key_w, preferred_element_type=jnp.float32)
        + b_key.astype(jnp.float32).T
    )
    value_pre = (
        jnp.einsum("sd,ehd->she", normed_in, value_w, preferred_element_type=jnp.float32)
        + value_b.astype(jnp.float32).T
    )
    seq_len, heads_local, head_dim = query_pre.shape
    kv_local = key_pre.shape[1]
    group_size = heads_local // kv_local
    score_scale = head_dim ** (-0.5)
    query_rot = (
        rotate(query_pre, 1.0).astype(jnp.bfloat16).reshape(seq_len, kv_local, group_size, head_dim)
    )
    key_rot = rotate(key_pre, 1.0).astype(jnp.bfloat16)
    value_low = value_pre.astype(jnp.bfloat16)
    row_index = lax.broadcasted_iota(jnp.int32, (seq_len, seq_len), 0)
    col_index = lax.broadcasted_iota(jnp.int32, (seq_len, seq_len), 1)
    allowed = (col_index <= row_index) | (col_index < prefix[0])

    def score_of():
        raw_scores = (
            jnp.einsum("skgd,tkd->kgst", query_rot, key_rot, preferred_element_type=jnp.float32)
            * score_scale
        )
        return jnp.where(allowed, raw_scores, NEG_BIG)

    scores = score_of()
    row_peak = jnp.max(scores, axis=-1, keepdims=True)
    shifted_exp = jnp.exp(scores - row_peak)
    row_total = jnp.sum(shifted_exp, axis=-1, keepdims=True)
    probs_low = (shifted_exp / row_total).astype(jnp.bfloat16)
    log_total = row_peak + jnp.log(row_total)
    attended = jnp.einsum(
        "kgst,tkd->skgd", probs_low, value_low, preferred_element_type=jnp.float32
    )
    attended_low = attended.reshape(seq_len, heads_local, head_dim).astype(jnp.bfloat16)
    attn_part = jnp.einsum("she,ehd->sd", attended_low, out_w, preferred_element_type=jnp.float32)
    middle = tok_float + lax.psum(attn_part, "tensor")
    gain_two, gate_w, up_w, down_w = (
        lax.all_gather(g_mlp, "dp", axis=0, tiled=True),
        lax.all_gather(w_gate, "dp", axis=0, tiled=True),
        lax.all_gather(w_up, "dp", axis=0, tiled=True),
        lax.all_gather(w_down, "dp", axis=0, tiled=True),
    )
    gain_mid = gain_two.astype(jnp.float32)
    normed_mid = normed(middle, gain_mid).astype(jnp.bfloat16)
    contract = (((1,), (1,)), ((), ()))
    rows_first = (((0,), (0,)), ((), ()))
    gate_val = lax.dot_general(normed_mid, gate_w, contract, preferred_element_type=jnp.float32)
    up_val = lax.dot_general(normed_mid, up_w, contract, preferred_element_type=jnp.float32)
    sigmoid_gate = jax.nn.sigmoid(gate_val)
    silu_gate = gate_val * sigmoid_gate
    hidden = (silu_gate * up_val).astype(jnp.bfloat16)
    mlp_part = jnp.dot(hidden, down_w, preferred_element_type=jnp.float32)
    result = middle + lax.psum(mlp_part.astype(jnp.bfloat16), "tensor").astype(jnp.float32)
    out_tokens = result.astype(jnp.bfloat16)
    gain_two, gate_w, up_w, down_w = (
        lax.all_gather(g_mlp, "dp", axis=0, tiled=True),
        lax.all_gather(w_gate, "dp", axis=0, tiled=True),
        lax.all_gather(w_up, "dp", axis=0, tiled=True),
        lax.all_gather(w_down, "dp", axis=0, tiled=True),
    )
    cot_float = cotangent.astype(jnp.float32)
    grad_wdown = lax.dot_general(hidden, cotangent, rows_first, preferred_element_type=jnp.float32)
    grad_hidden = lax.dot_general(cotangent, down_w, contract, preferred_element_type=jnp.float32)
    grad_gate = (
        grad_hidden * up_val * sigmoid_gate * (1.0 + gate_val * (1.0 - sigmoid_gate))
    ).astype(jnp.bfloat16)
    grad_up = (grad_hidden * silu_gate).astype(jnp.bfloat16)
    grad_wgate = lax.dot_general(
        grad_gate, normed_mid, rows_first, preferred_element_type=jnp.float32
    )
    grad_wup = lax.dot_general(grad_up, normed_mid, rows_first, preferred_element_type=jnp.float32)
    mid_part = jnp.dot(grad_gate, gate_w, preferred_element_type=jnp.float32) + jnp.dot(
        grad_up, up_w, preferred_element_type=jnp.float32
    )
    grad_normed_mid = lax.psum(mid_part, "tensor")
    unused_mid, pull_mid = jax.vjp(normed, middle, gain_mid)
    grad_mid_norm, grad_gmlp = pull_mid(grad_normed_mid)
    grad_middle = cot_float + grad_mid_norm
    gain_one, query_w, query_b, key_w, value_w, value_b, out_w = (
        lax.all_gather(g_attn, "dp", axis=0, tiled=True),
        lax.all_gather(w_query, "dp", axis=0, tiled=True),
        lax.all_gather(b_query, "dp", axis=0, tiled=True),
        lax.all_gather(w_key, "dp", axis=0, tiled=True),
        lax.all_gather(w_value, "dp", axis=0, tiled=True),
        lax.all_gather(b_value, "dp", axis=0, tiled=True),
        lax.all_gather(w_out, "dp", axis=0, tiled=True),
    )
    middle_low = grad_middle.astype(jnp.bfloat16)
    grad_wout = jnp.einsum(
        "she,sd->ehd", attended_low, middle_low, preferred_element_type=jnp.float32
    )
    grad_attended = (
        jnp.einsum("sd,ehd->she", middle_low, out_w, preferred_element_type=jnp.float32)
        .astype(jnp.bfloat16)
        .reshape(seq_len, kv_local, group_size, head_dim)
    )
    probs_again = jnp.exp(score_of() - log_total)
    again_low = probs_again.astype(jnp.bfloat16)
    grad_value = jnp.einsum(
        "kgst,skgd->tkd", again_low, grad_attended, preferred_element_type=jnp.float32
    ).astype(jnp.bfloat16)
    grad_probs = jnp.einsum(
        "skgd,tkd->kgst", grad_attended, value_low, preferred_element_type=jnp.float32
    )
    inner_sum = jnp.sum(probs_again * grad_probs, axis=-1, keepdims=True)
    grad_scores = (probs_again * (grad_probs - inner_sum)).astype(jnp.bfloat16)
    grad_qrot = (
        jnp.einsum(
            "kgst,tkd->skgd", grad_scores, key_rot, preferred_element_type=jnp.float32
        ).reshape(seq_len, heads_local, head_dim)
        * score_scale
    )
    grad_krot = (
        jnp.einsum("kgst,skgd->tkd", grad_scores, query_rot, preferred_element_type=jnp.float32)
        * score_scale
    )
    grad_query = rotate(grad_qrot, -1.0).astype(jnp.bfloat16)
    grad_key = rotate(grad_krot, -1.0).astype(jnp.bfloat16)
    grad_wquery = jnp.einsum(
        "she,sd->ehd", grad_query, normed_in, preferred_element_type=jnp.float32
    )
    grad_bquery = jnp.sum(grad_query.astype(jnp.float32), axis=0).T
    grad_wkey = jnp.einsum("she,sd->ehd", grad_key, normed_in, preferred_element_type=jnp.float32)
    grad_bkey = jnp.sum(grad_key.astype(jnp.float32), axis=0).T
    key_bias_total = lax.psum(grad_bkey, "dp")
    grad_wvalue = jnp.einsum(
        "she,sd->ehd", grad_value, normed_in, preferred_element_type=jnp.float32
    )
    grad_bvalue = jnp.sum(grad_value.astype(jnp.float32), axis=0).T
    in_part = jnp.einsum("she,ehd->sd", grad_query, query_w, preferred_element_type=jnp.float32)
    in_part = in_part + jnp.einsum(
        "she,ehd->sd", grad_key, key_w, preferred_element_type=jnp.float32
    )
    in_part = in_part + jnp.einsum(
        "she,ehd->sd", grad_value, value_w, preferred_element_type=jnp.float32
    )
    grad_normed_in = lax.psum(in_part.astype(jnp.bfloat16), "tensor").astype(jnp.float32)
    unused_in, pull_in = jax.vjp(normed, tok_float, gain_in)
    grad_in_norm, grad_gattn = pull_in(grad_normed_in)
    grad_tokens = grad_middle + grad_in_norm
    every_sum = (
        lax.psum_scatter(grad_gattn, "dp", scatter_dimension=0, tiled=True),
        lax.psum_scatter(grad_wquery, "dp", scatter_dimension=0, tiled=True),
        lax.psum_scatter(grad_bquery, "dp", scatter_dimension=0, tiled=True),
        lax.psum_scatter(grad_wkey, "dp", scatter_dimension=0, tiled=True),
        lax.psum_scatter(grad_wvalue, "dp", scatter_dimension=0, tiled=True),
        lax.psum_scatter(grad_bvalue, "dp", scatter_dimension=0, tiled=True),
        lax.psum_scatter(grad_wout, "dp", scatter_dimension=0, tiled=True),
        lax.psum_scatter(grad_gmlp, "dp", scatter_dimension=0, tiled=True),
        lax.psum_scatter(grad_wgate, "dp", scatter_dimension=0, tiled=True),
        lax.psum_scatter(grad_wup, "dp", scatter_dimension=0, tiled=True),
        lax.psum_scatter(grad_wdown, "dp", scatter_dimension=0, tiled=True),
    )
    attn_grads = every_sum[:7]
    mlp_grads = every_sum[7:]
    return (
        out_tokens,
        grad_tokens,
        attn_grads[0],
        attn_grads[1],
        attn_grads[2],
        attn_grads[3],
        key_bias_total,
        attn_grads[4],
        attn_grads[5],
        attn_grads[6],
        mlp_grads[0],
        mlp_grads[1],
        mlp_grads[2],
        mlp_grads[3],
    )


MESH = pl.DeviceIdType.MESH
BF = jnp.bfloat16
F32 = jnp.float32
NT = (((1,), (1,)), ((), ()))
NN = (((1,), (0,)), ((), ()))
TN = (((0,), (0,)), ((), ()))
VMEM_LIMIT = 67043328
ANY = pl.BlockSpec(memory_space=pl.ANY)
VM = pl.BlockSpec(memory_space=pltpu.VMEM)


def dot(a, b, dims):
    return lax.dot_general(a, b, dims, preferred_element_type=F32)


class Spot:
    def __init__(self, nz):
        self.nz = nz
        self.dp = lax.axis_index("dp")
        self.t = lax.axis_index("tensor")
        self.z, self.x, self.c = self.dp // 4, (self.dp // 2) % 2, self.dp % 2
        self.xn = (self.index(self.z, 1 - self.x, self.c), self.t)
        self.cn = (self.index(self.z, self.x, 1 - self.c), self.t)
        self.yn = (self.dp, 1 - self.t)

    def index(self, z, x, c):
        return (z * 2 + x) * 2 + c

    def near(self, k):
        nz, z = self.nz, self.z
        edge = jnp.minimum(z, nz - 1 - z)
        side = jnp.where(z <= nz - 1 - z, -1, 1)
        half = (k + 1) // 2
        close = side * half if k % 2 else -side * half
        return z + jnp.where(k <= 2 * edge, close, -side * (k - edge))

    def step(self, way):
        z = jnp.clip(self.z + way, 0, self.nz - 1)
        return (self.index(z, self.x, self.c), self.t)


class Wires:
    def __init__(self):
        self.sent = []

    def send(self, src, dst, send_sem, recv_sem, device, only=None):
        copy = pltpu.make_async_remote_copy(
            src_ref=src,
            dst_ref=dst,
            send_sem=send_sem,
            recv_sem=recv_sem,
            device_id=device,
            device_id_type=MESH,
        )
        if only is None:
            copy.start()
        else:
            pl.when(only)(copy.start)
        self.sent.append((copy, only))

    def landed(self, dst, recv_sem, spot):
        pltpu.make_async_remote_copy(
            src_ref=dst,
            dst_ref=dst,
            send_sem=recv_sem,
            recv_sem=recv_sem,
            device_id=spot.xn,
            device_id_type=MESH,
        ).wait_recv()

    def drain(self):
        for copy, only in self.sent:
            if only is None:
                copy.wait_send()
            else:
                pl.when(only)(copy.wait_send)
        self.sent = []


class Gather:
    def __init__(self, at, wires, slot, recv, send, core=None):
        self.at, self.wires, self.slot, self.recv, self.send, self.core = at, wires, slot, recv, send, core

    def hand(self, src, z, x, lane, device, only=None):
        self.wires.send(src, self.slot(z, x), self.send.at[lane], self.recv.at[z, x], device, only)

    def to_core(self, src, z, x, lane, only=None):
        if self.core is not None:
            slot, recv, send = self.core
            self.wires.send(src, slot(z, x), send.at[lane], recv.at[z, x], self.at.cn, only)

    def start(self, src):
        at = self.at
        self.hand(src, at.z, at.x, 0, at.step(1), at.z < at.nz - 1)
        self.hand(src, at.z, at.x, 1, at.step(-1), at.z > 0)
        self.hand(src, at.z, at.x, 2, at.xn)
        self.to_core(src, at.z, at.x, 0)

    def relay(self, k):
        at = self.at
        for side, way in ((0, 1), (1, -1)):
            z = at.z - way * k
            real = (z >= 0) & (z < at.nz)
            block = self.slot(z, at.x)
            pl.when(real)(functools.partial(self.wires.landed, block, self.recv.at[z, at.x], at))
            lane = 3 * k + side * 3 * (at.nz - 1)
            ahead = at.z + way
            self.hand(block, z, at.x, lane, at.step(way), real & (ahead >= 0) & (ahead < at.nz))
            self.hand(block, z, at.x, lane + 1, at.xn, real)
            self.to_core(block, z, at.x, k + side * (at.nz - 1), real)

    def column(self, k):
        at = self.at
        z = at.near(k)
        block = self.slot(z, 1 - at.x)
        self.wires.landed(block, self.recv.at[z, 1 - at.x], at)
        self.to_core(block, z, 1 - at.x, 2 * at.nz - 1 + k)

    @staticmethod
    def lanes(nz):
        return 3 + 6 * (nz - 1)

    @staticmethod
    def core_lanes(nz):
        return 3 * nz - 1


class LineSum:
    def __init__(self, at, wires, inbox, outbox, recv, send):
        self.at, self.wires, self.inbox, self.outbox, self.recv, self.send = at, wires, inbox, outbox, recv, send

    def add(self, way, s, acc_ref, real):
        at = self.at

        def go():
            self.wires.landed(self.inbox.at[way, s], self.recv.at[way, s], at)
            acc_ref[...] += self.inbox[way, s].astype(F32)

        pl.when(real)(go)

    def push(self, k, acc_ref, only=None, again=False):
        at = self.at
        s = at.near(k)
        up = s > at.z
        way = jnp.where(up, 0, 1)
        target = at.step(jnp.where(up, 1, -1))

        def fill():
            self.add(way, s, acc_ref, (up & (at.z > 0)) | ((s < at.z) & (at.z < at.nz - 1)))
            self.outbox[k] = acc_ref[...].astype(BF)

        fill() if only is None else pl.when(only)(fill)
        self.wires.send(
            self.outbox.at[k], self.inbox.at[way, s], self.send.at[k], self.recv.at[way, s], target, only
        )
        if only is not None:
            copy, _ = self.wires.sent.pop()
            if not again:
                self.wires.sent.append((copy, None))

    def close(self, acc_ref):
        at = self.at
        self.add(0, at.z, acc_ref, at.z > 0)
        self.add(1, at.z, acc_ref, at.z < at.nz - 1)


class OwnerSum:
    def __init__(self, at, wires, full, rows, bufs, sems):
        self.at, self.wires, self.full, self.rows = at, wires, full, rows
        self.core_out, self.core_in, self.x_out, self.x_in, outbox, inbox, self.acc = bufs
        self.a_recv, self.a_send, self.x_recv, self.x_send, z_recv, z_send = sems
        self.line = LineSum(at, wires, inbox, outbox, z_recv, z_send)
        self.order = list(range(at.nz - 1, -1, -1))

    @staticmethod
    def buffers(nz, units, rows, wide):
        block = (units * rows, wide)
        vm = pltpu.VMEM
        return [
            vm((nz, 2) + block, BF),
            vm((nz, 2) + block, BF),
            vm((nz,) + block, BF),
            vm((nz,) + block, BF),
            vm((nz,) + block, BF),
            vm((2, nz) + block, BF),
            vm(block, F32),
        ]

    @staticmethod
    def semaphores(nz):
        dma = pltpu.SemaphoreType.DMA
        return [dma((nz, 2)), dma((nz, 2)), dma((nz,)), dma((nz,)), dma((2, nz)), dma((nz,))]

    def terms(self, z, x, c):
        start = pl.multiple_of(self.at.index(z, x, c) * self.rows, self.rows)
        piece = self.full[:, pl.ds(start, self.rows), :]
        return piece.reshape(piece.shape[0] * self.rows, piece.shape[2])

    def to_core(self):
        at = self.at
        for far in (1, 0):
            for k in self.order:
                x = 1 - at.x if far else at.x
                self.core_out[k, far] = self.terms(at.near(k), x, 1 - at.c).astype(BF)
                self.wires.send(
                    self.core_out.at[k, far],
                    self.core_in.at[k, far],
                    self.a_send.at[k, far],
                    self.a_recv.at[k, far],
                    at.cn,
                )

    def across(self):
        at = self.at
        for k in self.order:
            self.wires.landed(self.core_in.at[k, 1], self.a_recv.at[k, 1], at)
            both = self.terms(at.near(k), 1 - at.x, at.c) + self.core_in[k, 1].astype(F32)
            self.x_out[k] = both.astype(BF)
            self.wires.send(self.x_out.at[k], self.x_in.at[k], self.x_send.at[k], self.x_recv.at[k], at.xn)

    def along(self, out):
        at = self.at
        for k in self.order:
            self.wires.landed(self.core_in.at[k, 0], self.a_recv.at[k, 0], at)
            self.wires.landed(self.x_in.at[k], self.x_recv.at[k], at)
            acc = self.acc if k else out
            acc[...] = (
                self.terms(at.near(k), at.x, at.c)
                + self.core_in[k, 0].astype(F32)
                + self.x_in[k].astype(F32)
            )
            if k:
                self.line.push(k, acc)

    def close(self, out):
        self.line.close(out)


def greet(at, devices, line=True):
    barrier = pltpu.get_barrier_semaphore()

    def hello(device):
        pl.semaphore_signal(barrier, inc=1, device_id=device, device_id_type=MESH)

    for device in devices:
        hello(device)
    count = len(devices)
    if line:
        up, down = at.z < at.nz - 1, at.z > 0
        pl.when(up)(functools.partial(hello, at.step(1)))
        pl.when(down)(functools.partial(hello, at.step(-1)))
        count = count + jnp.where(up, 1, 0) + jnp.where(down, 1, 0)
    pl.semaphore_wait(barrier, count)


def gather_kernel(
    nz,
    qkv_in,
    wo_in,
    small_in,
    cot_in,
    gate_in,
    up_in,
    down_in,
    qkv,
    wo,
    small,
    cot,
    mlp_w,
    stage_a,
    stage_b,
    stage_c,
    local_sem,
    q_recv,
    q_send,
    q_core_recv,
    q_core_send,
    o_recv,
    o_send,
    o_core_recv,
    o_core_send,
    s_recv,
    s_send,
    c_recv,
    c_send,
    w_recv,
    w_send,
):
    at = Spot(nz)
    ndp = 4 * nz
    half = cot_in.shape[0] // 2
    rows = qkv_in.shape[1]
    others = [(lax.rem(at.dp + p, ndp), at.t) for p in range(1, ndp)]
    greet(at, others + [at.yn], line=False)
    wires = Wires()

    def part(ref, core):
        def slot(z, x):
            owner = at.index(z, x, core)
            return ref.at[:, pl.ds(pl.multiple_of(owner * rows, rows), rows), :]

        return slot

    def cot_slot(z, x):
        return cot.at[z, x]

    q_slot, o_slot = part(qkv, at.c), part(wo, at.c)
    gq = Gather(at, wires, q_slot, q_recv, q_send, (q_slot, q_core_recv, q_core_send))
    go = Gather(at, wires, o_slot, o_recv, o_send, (o_slot, o_core_recv, o_core_send))
    gc = Gather(at, wires, cot_slot, c_recv, c_send)
    gq.start(qkv_in)
    go.start(wo_in)
    mine = at.c * 2 + at.t
    for i, src in enumerate((gate_in, up_in, down_in)):
        wires.send(src, mlp_w.at[i, mine], w_send.at[0, i], w_recv.at[i, mine], at.yn)
        wires.send(src, mlp_w.at[i, mine], w_send.at[1, i], w_recv.at[i, mine], at.cn)
    for p, device in enumerate(others):
        wires.send(small_in, small.at[at.dp], s_send.at[p], s_recv.at[at.dp], device)
    loads = [
        pltpu.make_async_copy(qkv_in, stage_a, local_sem.at[0]),
        pltpu.make_async_copy(wo_in, stage_b, local_sem.at[1]),
        pltpu.make_async_copy(small_in, stage_c, local_sem.at[2]),
    ]
    stores = [
        pltpu.make_async_copy(stage_a, q_slot(at.z, at.x), local_sem.at[3]),
        pltpu.make_async_copy(stage_b, o_slot(at.z, at.x), local_sem.at[4]),
        pltpu.make_async_copy(stage_c, small.at[at.dp], local_sem.at[5]),
    ]
    for load in loads:
        load.start()
    for load, store in zip(loads, stores):
        load.wait()
        store.start()
    for k in range(1, nz):
        gq.relay(k)
        go.relay(k)
    gc.start(cot_in.at[pl.ds(pl.multiple_of(at.t * half, half), half), :])
    for k in range(nz):
        gq.column(k)
        go.column(k)
    for k in range(1, nz):
        gc.relay(k)
    for k in range(nz):
        gc.column(k)
    across = at.c * 2 + 1 - at.t
    for i in range(3):
        wires.landed(mlp_w.at[i, across], w_recv.at[i, across], at)
        wires.send(mlp_w.at[i, across], mlp_w.at[i, across], w_send.at[2, i], w_recv.at[i, across], at.cn)
    for i in range(3):
        for tt in range(2):
            there = (1 - at.c) * 2 + tt
            wires.landed(mlp_w.at[i, there], w_recv.at[i, there], at)
    for device in others:
        wires.landed(small.at[device[0]], s_recv.at[device[0]], at)
    for ref, recv in ((qkv, q_core_recv), (wo, o_core_recv)):
        slot = part(ref, 1 - at.c)
        for z in range(nz):
            for x in range(2):
                wires.landed(slot(z, x), recv.at[z, x], at)
    for store in stores:
        store.wait()
    wires.drain()


def gather_weights(nz, qkv, wo, small, cotangent, gate, up, down):
    ndp = 4 * nz
    half, wide = cotangent.shape[0] // 2, cotangent.shape[1]
    shape = jax.ShapeDtypeStruct
    dma = pltpu.SemaphoreType.DMA
    return pl.pallas_call(
        functools.partial(gather_kernel, nz),
        out_shape=(
            shape((qkv.shape[0], ndp * qkv.shape[1], wide), BF),
            shape((wo.shape[0], ndp * wo.shape[1], wide), BF),
            shape((ndp,) + small.shape, BF),
            shape((nz, 2, half, wide), BF),
            shape((3, 4) + gate.shape, BF),
        ),
        in_specs=[ANY] * 7,
        out_specs=[ANY] * 5,
        scratch_shapes=[
            pltpu.VMEM(qkv.shape, BF),
            pltpu.VMEM(wo.shape, BF),
            pltpu.VMEM(small.shape, BF),
            dma((6,)),
            dma((nz, 2)),
            dma((Gather.lanes(nz),)),
            dma((nz, 2)),
            dma((Gather.core_lanes(nz),)),
            dma((nz, 2)),
            dma((Gather.lanes(nz),)),
            dma((nz, 2)),
            dma((Gather.core_lanes(nz),)),
            dma((ndp,)),
            dma((ndp,)),
            dma((nz, 2)),
            dma((Gather.lanes(nz),)),
            dma((3, 4)),
            dma((3, 3)),
        ],
        compiler_params=pltpu.CompilerParams(
            collective_id=1, has_side_effects=True, vmem_limit_bytes=VMEM_LIMIT
        ),
        name="gather_weights",
    )(qkv, wo, small, cotangent, gate, up, down)


def mlp_kernel(
    nz,
    tok_in,
    part_in,
    gain_in,
    cot_in,
    mlp_in,
    cot_own_in,
    gate_in,
    up_in,
    down_in,
    out_part,
    keep_gate,
    keep_up,
    keep_down,
    give,
    grad_half,
    mid_half,
    gain_send,
    weights,
    cot,
    nm,
    gh,
    hid,
    gg,
    gu,
    own,
    xs,
    xr,
    z_in,
    pair,
    grads,
    partner,
    ysend,
    yrecv,
    down_send,
    down_recv,
    local_sem,
    n_recv,
    n_send,
    x_recv,
    x_send,
    z_recv,
    z_send,
    p_recv,
    p_send,
    y_recv,
    y_send,
):
    at = Spot(nz)
    half, wide = nm.shape[2], nm.shape[3]
    two = 2 * half
    shard = mlp_in.shape[2]
    padded = weights.shape[2]
    units = 4 * padded
    wires = Wires()
    mine = at.c * 2 + at.t

    loads = []

    def load(src, dst, sem):
        copy = pltpu.make_async_copy(src, dst, sem)
        copy.start()
        loads.append(copy)
        return copy

    per = [[], [], []]
    for i, src in ((2, down_in), (0, gate_in), (1, up_in)):
        per[i].append(load(src, weights.at[i, mine, pl.ds(0, shard)], local_sem.at[i * 4]))
        for j, slot in enumerate((at.c * 2 + 1 - at.t, (1 - at.c) * 2, (1 - at.c) * 2 + 1)):
            per[i].append(
                load(mlp_in.at[i, slot], weights.at[i, slot, pl.ds(0, shard)], local_sem.at[i * 4 + 1 + j])
            )
    cot_loads = [
        load(
            cot_own_in.at[pl.ds(pl.multiple_of(at.t * half, half), half), :],
            cot.at[at.z, at.x],
            local_sem.at[12],
        )
    ]
    for k in range(nz):
        zk = at.near(k)
        if k:
            cot_loads.append(load(cot_in.at[zk, at.x], cot.at[zk, at.x], local_sem.at[12 + 2 * k]))
        cot_loads.append(load(cot_in.at[zk, 1 - at.x], cot.at[zk, 1 - at.x], local_sem.at[13 + 2 * k]))
    for i in range(3):
        for s in range(4):
            weights[i, s, shard:padded, :] = jnp.zeros((padded - shard, wide), BF)

    far_row = pl.multiple_of((1 - at.t) * half, half)
    own_row = pl.multiple_of(at.t * half, half)
    greet(at, [at.xn, at.yn, at.cn])
    ysend[...] = part_in[pl.ds(far_row, half), :].astype(BF)
    wires.send(ysend, yrecv, y_send.at[0], y_recv.at[0], at.yn)
    for copy in per[2] + cot_loads:
        copy.wait()
    down_w = weights.at[2]

    for k in range(nz):
        zk = at.near(k)
        gh[zk] = dot(cot[zk].reshape(two, wide), down_w[...].reshape(units, wide), NT)

    wires.landed(yrecv, y_recv.at[0], at)
    middle = (
        tok_in[pl.ds(own_row, half), :].astype(F32)
        + part_in[pl.ds(own_row, half), :]
        + yrecv[...].astype(F32)
    )
    gain = gain_in[...]
    rms = lax.rsqrt(jnp.mean(middle * middle, axis=-1, keepdims=True) + EPS)
    mid_half[...] = middle
    nm[at.z, at.x] = (middle * rms * gain).astype(BF)

    def nm_slot(z, x):
        return nm.at[z, x]

    gather = Gather(at, wires, nm_slot, n_recv, n_send)
    line = LineSum(at, wires, z_in, xr, z_recv, z_send)
    at_end = (at.z == 0) | (at.z == nz - 1)
    gather.start(nm.at[at.z, at.x])
    for copy in per[0] + per[1]:
        copy.wait()
    gate_w, up_w = weights.at[0], weights.at[1]

    def hand_over(k):
        wires.send(xs.at[k], xr.at[k], x_send.at[k], x_recv.at[k], at.xn)

    def column_sum(k):
        wires.landed(xr.at[k], x_recv.at[k], at)
        own[k] += xr[k].astype(F32)
        if k:
            line.push(k, own.at[k], only=at_end)

    if nz > 1:
        gather.relay(1)
    for k in range(nz):
        zk = at.near(k)
        gather.column(k)
        a = nm[zk].reshape(two, wide)
        gate = dot(a, gate_w[...].reshape(units, wide), NT)
        up = dot(a, up_w[...].reshape(units, wide), NT)
        sig = jax.nn.sigmoid(gate)
        silu = gate * sig
        hid[zk] = (silu * up).astype(BF)
        ghk = gh[zk]
        gg[zk] = (ghk * up * sig * (1.0 + gate * (1.0 - sig))).astype(BF)
        gu[zk] = (ghk * silu).astype(BF)
        if k + 2 < nz:
            gather.relay(k + 2)
        pair[...] = (
            dot(gg[zk], gate_w[...].reshape(units, wide), NN)
            + dot(gu[zk], up_w[...].reshape(units, wide), NN)
        ).reshape(2, half, wide)
        xs[k] = pair[1 - at.x].astype(BF)
        own[k] = pair[at.x]
        if k:
            hand_over(k)
        if k > 1:
            column_sum(k - 1)
    hand_over(0)
    tile = 512

    def weight_grad(i, lhs, rhs):
        left = lhs[...].reshape(nz * two, units)
        for j in range(wide // tile):
            cols = slice(j * tile, (j + 1) * tile)
            right = rhs[:, :, :, cols].reshape(nz * two, tile)
            acc = dot(left, right, TN).astype(BF).reshape(4, padded, tile)
            grads[i, :, :, cols] = acc[:, :shard]
        for j in range(2):
            wires.send(
                grads.at[i, (1 - at.c) * 2 + j], partner.at[i, j], p_send.at[i, j], p_recv.at[i, j], at.cn
            )

    def chip_sum(i, kept, given):
        for j in range(2):
            wires.landed(partner.at[i, j], p_recv.at[i, j], at)
        kept[...] = grads[i, mine].astype(F32) + partner[i, at.t].astype(F32)
        given[...] = (
            grads[i, at.c * 2 + 1 - at.t].astype(F32) + partner[i, 1 - at.t].astype(F32)
        ).astype(BF)

    weight_grad(2, hid, cot)
    for k in range(nz):
        zk = at.near(k)
        out_part[zk] = dot(hid[zk], down_w[...].reshape(units, wide), NN).astype(BF).reshape(2, half, wide)
    chip_sum(2, keep_down, down_send)
    wires.send(down_send, down_recv, y_send.at[1], y_recv.at[1], at.yn)
    column_sum(nz - 1)
    for k in [nz - 2, nz - 1] + list(range(nz - 3, 0, -1)):
        line.push(k, own.at[k], only=jnp.logical_not(at_end), again=True)
    weight_grad(0, gg, nm)
    weight_grad(1, gu, nm)
    column_sum(0)
    line.close(own.at[0])
    total = own[0]
    middle = mid_half[...]
    rms = lax.rsqrt(jnp.mean(middle * middle, axis=-1, keepdims=True) + EPS)
    unit = middle * rms
    gain_send[...] = jnp.sum(total * unit, axis=0, keepdims=True)
    scaled = total * gain
    cot_f = cot[at.z, at.x].astype(F32)
    grad_mid = cot_f + rms * (scaled - unit * jnp.mean(scaled * unit, axis=-1, keepdims=True))
    grad_half[...] = grad_mid.astype(BF)
    chip_sum(0, keep_gate, give.at[0])
    chip_sum(1, keep_up, give.at[1])
    wires.landed(down_recv, y_recv.at[1], at)
    keep_down[...] += down_recv[...].astype(F32)
    wires.drain()


def mlp_step(nz, tokens, part, gain, cot_all, mlp_all, cotangent, gate, up, down):
    half, wide = cotangent.shape[0] // 2, cotangent.shape[1]
    shard = gate.shape[0]
    padded = -(-shard // 32) * 32
    units = 4 * padded
    shape = jax.ShapeDtypeStruct
    dma = pltpu.SemaphoreType.DMA
    vm = pltpu.VMEM
    return pl.pallas_call(
        functools.partial(mlp_kernel, nz),
        out_shape=(
            shape((nz, 2, half, wide), BF),
            shape((shard, wide), F32),
            shape((shard, wide), F32),
            shape((shard, wide), F32),
            shape((2, shard, wide), BF),
            shape((half, wide), BF),
            shape((half, wide), F32),
            shape((1, wide), F32),
        ),
        in_specs=[VM, VM, VM] + [ANY] * 6,
        out_specs=[VM] * 8,
        scratch_shapes=[
            vm((3, 4, padded, wide), BF),
            vm((nz, 2, half, wide), BF),
            vm((nz, 2, half, wide), BF),
            vm((nz, 2 * half, units), F32),
            vm((nz, 2 * half, units), BF),
            vm((nz, 2 * half, units), BF),
            vm((nz, 2 * half, units), BF),
            vm((nz, half, wide), F32),
            vm((nz, half, wide), BF),
            vm((nz, half, wide), BF),
            vm((2, nz, half, wide), BF),
            vm((2, half, wide), F32),
            vm((3, 4, shard, wide), BF),
            vm((3, 2, shard, wide), BF),
            vm((half, wide), BF),
            vm((half, wide), BF),
            vm((shard, wide), BF),
            vm((shard, wide), BF),
            dma((12 + 2 * nz + 2,)),
            dma((nz, 2)),
            dma((Gather.lanes(nz),)),
            dma((nz,)),
            dma((nz,)),
            dma((2, nz)),
            dma((nz,)),
            dma((3, 2)),
            dma((3, 2)),
            dma((2,)),
            dma((2,)),
        ],
        compiler_params=pltpu.CompilerParams(
            collective_id=2, has_side_effects=True, vmem_limit_bytes=VMEM_LIMIT
        ),
        name="mlp_step",
    )(tokens, part, gain, cot_all, mlp_all, cotangent, gate, up, down)


def turn(field, cos, sin):
    return field * cos + pltpu.roll(field, field.shape[-1] // 2, 1) * sin


def tail_kernel(
    nz,
    scale,
    out_part,
    mid_half,
    grad_half,
    gain_part,
    att,
    q_rot,
    kv,
    probs,
    nm_in,
    tok_in,
    gain_in,
    cos_in,
    sin_in,
    qkv_in,
    wo_in,
    give,
    gq,
    go,
    out_tokens,
    grad_tokens,
    small,
    got,
    mid_low,
    gain_got,
    qkv_w,
    out_w,
    full_q,
    full_o,
    ga,
    gs,
    gpre,
    in_part,
    in_got,
    b_x,
    b_out,
    b_in,
    b_acc,
    out_send,
    out_got,
    small_all,
    local_sem,
    b_xrecv,
    b_xsend,
    b_zrecv,
    b_zsend,
    y_recv,
    y_send,
    s_recv,
    s_send,
    *owner_refs,
):
    at = Spot(nz)
    ndp = 4 * nz
    half, wide = mid_half.shape
    seq = 2 * half
    heads, head_dim = full_o.shape[:2]
    rows = head_dim // ndp
    others = [(lax.rem(at.dp + p, ndp), at.t) for p in range(1, ndp)]
    loads = [
        pltpu.make_async_copy(wo_in, out_w, local_sem.at[0]),
        pltpu.make_async_copy(qkv_in, qkv_w, local_sem.at[1]),
    ]
    for load in loads:
        load.start()
    greet(at, others + [at.yn], line=False)
    wires = Wires()
    sum_q = OwnerSum(at, wires, full_q, rows, owner_refs[:7], owner_refs[14:20])
    sum_o = OwnerSum(at, wires, full_o, rows, owner_refs[7:14], owner_refs[20:26])
    out_line = LineSum(at, wires, b_in, b_out, b_zrecv, b_zsend)

    def swap_y(i, src, dst):
        wires.send(src, dst, y_send.at[i], y_recv.at[i], at.yn)

    def out_across(ks):
        for k in ks:
            wires.send(out_part.at[at.near(k), 1 - at.x], b_x.at[k], b_xsend.at[k], b_xrecv.at[k], at.xn)

    def out_along(ks):
        for k in ks:
            wires.landed(b_x.at[k], b_xrecv.at[k], at)
            b_acc[...] = out_part[at.near(k), at.x].astype(F32) + b_x[k].astype(F32)
            if k:
                out_line.push(k, b_acc)

    far, close = list(range(nz - 1, 1, -1)), [1, 0]
    swap_y(0, grad_half, mid_low.at[at.t])
    swap_y(1, gain_part, gain_got)
    out_across(far)
    mid_low[at.t] = grad_half[...]
    wires.landed(mid_low.at[1 - at.t], y_recv.at[0], at)
    swap_y(2, give.at[0], got.at[0])
    loads[0].wait()
    low = mid_low[...].reshape(seq, wide)
    att_grad = dot(low, out_w[...].reshape(heads * head_dim, wide), NT).astype(BF)
    for h in range(heads):
        ga[h] = att_grad[:, h * head_dim : (h + 1) * head_dim]
    tile = 512

    def weight_grad(full, lhs, rhs_of):
        for j in range(wide // tile):
            cols = slice(j * tile, (j + 1) * tile)
            full[:, :, cols] = dot(lhs, rhs_of(cols), TN).reshape(full.shape[0], head_dim, tile)

    weight_grad(full_o, att[...], lambda cols: mid_low[:, :, cols].reshape(seq, tile))
    sum_o.to_core()

    ga_all = ga[...].reshape(heads * seq, head_dim)
    p = probs[...].reshape(heads * seq, seq)
    key, value = kv[0], kv[1]
    grad_value = dot(p.astype(BF), ga_all, TN).astype(BF)
    grad_p = dot(ga_all, value, NT)
    inner = jnp.sum(p * grad_p, axis=-1, keepdims=True)
    gs[...] = (p * (grad_p - inner)).astype(BF)
    sum_o.across()
    cos, sin = cos_in[...], -sin_in[...]
    grad_q = dot(gs[...], key, NN) * scale
    for h in range(heads):
        gpre[:, h * head_dim : (h + 1) * head_dim] = turn(grad_q[h * seq : (h + 1) * seq], cos, sin).astype(BF)
    grad_k = dot(gs[...], q_rot[...].reshape(heads * seq, head_dim), TN) * scale
    gpre[:, heads * head_dim : (heads + 1) * head_dim] = turn(grad_k, cos, sin).astype(BF)
    gpre[:, (heads + 1) * head_dim :] = grad_value
    loads[1].wait()
    pre = gpre[...]
    in_part[...] = dot(pre, qkv_w[...].reshape((heads + 2) * head_dim, wide), NN).astype(BF)
    swap_y(3, in_part, in_got)
    swap_y(4, give.at[1], got.at[1])
    out_along(far)
    weight_grad(full_q, pre, lambda cols: nm_in[:, cols])
    sum_q.to_core()
    bias = jnp.sum(pre.astype(F32), axis=0, keepdims=True)
    sum_q.across()
    out_across(close)
    sum_o.along(go)
    wires.landed(in_got, y_recv.at[3], at)
    grad_in = in_part[...].astype(F32) + in_got[...].astype(F32)
    tok = tok_in[...].astype(F32)
    rms = lax.rsqrt(jnp.mean(tok * tok, axis=-1, keepdims=True) + EPS)
    unit = tok * rms
    grad_gain = jnp.sum(grad_in * unit, axis=0, keepdims=True)
    scaled = grad_in * gain_in[...]
    grad_tokens[...] = mid_low[...].reshape(seq, wide).astype(F32) + rms * (
        scaled - unit * jnp.mean(scaled * unit, axis=-1, keepdims=True)
    )
    wires.landed(gain_got, y_recv.at[1], at)
    gmlp = gain_part[...] + gain_got[...]
    lanes = small.shape[1]
    steps = wide // lanes
    for i in range(steps):
        small_all[at.dp, i : i + 1, :] = grad_gain[:, i * lanes : (i + 1) * lanes]
        small_all[at.dp, steps + i : steps + i + 1, :] = gmlp[:, i * lanes : (i + 1) * lanes]
    for i in range(bias.shape[1] // lanes):
        small_all[at.dp, 2 * steps + i : 2 * steps + i + 1, :] = bias[:, i * lanes : (i + 1) * lanes]
    for n, device in enumerate(others):
        wires.send(small_all.at[at.dp], small_all.at[at.dp], s_send.at[n], s_recv.at[at.dp], device)
    sum_q.along(gq)
    out_along(close)
    sum_o.close(go)
    sum_q.close(gq)
    out_line.close(b_acc)
    out_send[...] = (b_acc[...] + mid_half[...]).astype(BF)
    swap_y(5, out_send, out_got)
    out_tokens[at.t] = out_send[...]
    for device in others:
        wires.landed(small_all.at[device[0]], s_recv.at[device[0]], at)
    total = small_all[0]
    for n in range(1, ndp):
        total = total + small_all[n]
    small[...] = total
    for i in range(2):
        wires.landed(got.at[i], y_recv.at[2 + 2 * i], at)
    wires.landed(out_got, y_recv.at[5], at)
    out_tokens[1 - at.t] = out_got[...]
    wires.drain()


def tail_step(nz, scale, out_part, mid_half, grad_half, gain_part, att, q_rot, kv, probs, nm_in, tokens, gain, cos, sin, qkv, wo, give):
    ndp = 4 * nz
    half, wide = mid_half.shape
    seq = 2 * half
    heads, head_dim = wo.shape[:2]
    rows = head_dim // ndp
    shape = jax.ShapeDtypeStruct
    dma = pltpu.SemaphoreType.DMA
    vm = pltpu.VMEM
    lanes = wide // 3
    srows = 6 + (heads + 2) * head_dim // lanes
    return pl.pallas_call(
        functools.partial(tail_kernel, nz, scale),
        out_shape=(
            shape(((heads + 2) * rows, wide), F32),
            shape((heads * rows, wide), F32),
            shape((2, half, wide), BF),
            shape((seq, wide), F32),
            shape((srows, lanes), F32),
            shape(give.shape, BF),
        ),
        in_specs=[VM] * 13 + [ANY] * 3,
        out_specs=[VM] * 5 + [ANY],
        scratch_shapes=[
            vm((2, half, wide), BF),
            vm((1, wide), F32),
            vm(qkv.shape, BF),
            vm(wo.shape, BF),
            vm((heads + 2, head_dim, wide), F32),
            vm((heads, head_dim, wide), F32),
            vm((heads, seq, head_dim), BF),
            vm((heads * seq, seq), BF),
            vm((seq, (heads + 2) * head_dim), BF),
            vm((seq, wide), BF),
            vm((seq, wide), BF),
            vm((nz, half, wide), BF),
            vm((nz, half, wide), BF),
            vm((2, nz, half, wide), BF),
            vm((half, wide), F32),
            vm((half, wide), BF),
            vm((half, wide), BF),
            vm((ndp, srows, lanes), F32),
            dma((2,)),
            dma((nz,)),
            dma((nz,)),
            dma((2, nz)),
            dma((nz,)),
            dma((6,)),
            dma((6,)),
            dma((ndp,)),
            dma((ndp,)),
        ]
        + OwnerSum.buffers(nz, heads + 2, rows, wide)
        + OwnerSum.buffers(nz, heads, rows, wide)
        + OwnerSum.semaphores(nz)
        + OwnerSum.semaphores(nz),
        compiler_params=pltpu.CompilerParams(
            collective_id=3, has_side_effects=True, vmem_limit_bytes=VMEM_LIMIT
        ),
        name="tail_step",
    )(out_part, mid_half, grad_half, gain_part, att, q_rot, kv, probs, nm_in, tokens, gain, cos, sin, qkv, wo, give)


def rope_tables(seq_len, head_dim):
    half_dim = head_dim // 2
    places = np.arange(seq_len, dtype=np.float32)
    freqs = np.float32(ROPE_BASE) ** (-(np.arange(half_dim, dtype=np.float32) * np.float32(2.0) / np.float32(head_dim)))
    angles = places[:, None] * freqs[None, :]
    cos, sin = np.cos(angles), np.sin(angles)
    return (
        jnp.asarray(np.concatenate([cos, cos], axis=1), F32),
        jnp.asarray(np.concatenate([-sin, sin], axis=1), F32),
    )


def rotate_heads(field, flip_sign):
    half_dim = field.shape[-1] // 2
    places = jnp.arange(field.shape[1], dtype=F32)
    freqs = ROPE_BASE ** (-(jnp.arange(half_dim, dtype=F32) * 2.0 / field.shape[-1]))
    angles = places[:, None] * freqs[None, :]
    cosine = jnp.cos(angles)[None]
    sine = flip_sign * jnp.sin(angles)[None]
    first = field[..., :half_dim]
    second = field[..., half_dim:]
    return jnp.concatenate(
        [first * cosine - second * sine, second * cosine + first * sine], axis=-1
    )


def planes(
    tokens,
    prefix,
    g_attn,
    w_query,
    b_query,
    w_key,
    b_key,
    w_value,
    b_value,
    w_out,
    g_mlp,
    w_gate,
    w_up,
    w_down,
    cotangent,
    ndp,
):
    nz = ndp // 4
    seq_len, wide = tokens.shape
    rows, heads = b_query.shape
    head_dim = rows * ndp
    dp = lax.axis_index("dp")
    gshare = g_attn.shape[0]

    def heads_first(w):
        return jnp.swapaxes(w, 0, 1)

    qkv_own = jnp.concatenate([heads_first(w_query), heads_first(w_key), heads_first(w_value)], axis=0)
    wo_own = heads_first(w_out)

    def row(v):
        flat = v.reshape(1, -1)
        return jnp.pad(flat, ((0, 0), (0, 128 - flat.shape[1])))

    small_own = jnp.concatenate(
        [row(g_attn), row(g_mlp), row(b_query.T), row(b_value)] + [jnp.zeros((4, 128), BF)], axis=0
    )
    qkv_w, out_w, small, cot_all, mlp_all = gather_weights(
        nz, qkv_own, wo_own, small_own, cotangent, w_gate, w_up, w_down
    )
    gain_in = small[:, 0, :gshare].reshape(1, wide).astype(F32)
    gain_mid = small[:, 1, :gshare].reshape(1, wide).astype(F32)
    query_b = small[:, 2, : heads * rows].reshape(ndp, heads, rows).transpose(1, 0, 2).reshape(heads, 1, head_dim)
    value_b = small[:, 3, :rows].reshape(1, 1, head_dim)
    key_b = b_key.T.reshape(1, 1, head_dim)
    bias = jnp.concatenate([query_b, key_b, value_b], axis=0).astype(F32)

    tok_float = tokens.astype(F32)
    normed_in = normed(tok_float, gain_in).astype(BF)
    pre = jnp.einsum("sd,ked->kse", normed_in, qkv_w, preferred_element_type=F32) + bias
    score_scale = head_dim ** (-0.5)
    rot = rotate_heads(pre[: heads + 1], 1.0).astype(BF)
    query_rot, key_rot = rot[:heads], rot[heads]
    value_low = pre[heads + 1].astype(BF)
    row_index = lax.broadcasted_iota(jnp.int32, (seq_len, seq_len), 0)
    col_index = lax.broadcasted_iota(jnp.int32, (seq_len, seq_len), 1)
    allowed = (col_index <= row_index) | (col_index < prefix[0])
    raw_scores = jnp.einsum("gsd,td->gst", query_rot, key_rot, preferred_element_type=F32) * score_scale
    scores = jnp.where(allowed, raw_scores, NEG_BIG)
    row_peak = jnp.max(scores, axis=-1, keepdims=True)
    shifted_exp = jnp.exp(scores - row_peak)
    row_total = jnp.sum(shifted_exp, axis=-1, keepdims=True)
    probs = shifted_exp / row_total
    probs_low = probs.astype(BF)
    attended = jnp.einsum("gst,td->gsd", probs_low, value_low, preferred_element_type=F32)
    attended_low = attended.astype(BF)
    attn_part = jnp.einsum("gse,ged->sd", attended_low, out_w, preferred_element_type=F32)

    out_part, keep_gate, keep_up, keep_down, give, grad_half, mid_half, gain_part = mlp_step(
        nz, tokens, attn_part, gain_mid, cot_all, mlp_all, cotangent, w_gate, w_up, w_down
    )
    att = jnp.swapaxes(attended_low, 0, 1).reshape(seq_len, heads * head_dim)
    cos, sin = rope_tables(seq_len, head_dim)
    gq, go, out_tokens, grad_tokens, sums, got = tail_step(
        nz,
        score_scale,
        out_part,
        mid_half,
        grad_half,
        gain_part,
        att,
        query_rot,
        jnp.stack([key_rot, value_low]),
        probs,
        normed_in,
        tokens,
        gain_in,
        cos,
        sin,
        qkv_w,
        out_w,
        give,
    )
    gq = gq.reshape(heads + 2, rows, wide).transpose(1, 0, 2)
    go = go.reshape(heads, rows, wide).transpose(1, 0, 2)
    gattn_all = sums[:3].reshape(wide)
    gmlp_all = sums[3:6].reshape(wide)
    bias_all = sums[6:].reshape(heads + 2, head_dim).T
    bias_own = lax.dynamic_slice_in_dim(bias_all, dp * rows, rows, axis=0)
    return (
        out_tokens.reshape(seq_len, wide),
        grad_tokens,
        lax.dynamic_slice_in_dim(gattn_all, dp * gshare, gshare),
        gq[:, :heads],
        bias_own[:, :heads],
        gq[:, heads : heads + 1],
        bias_all[:, heads : heads + 1],
        gq[:, heads + 1 :],
        bias_own[:, heads + 1 :],
        go,
        lax.dynamic_slice_in_dim(gmlp_all, dp * gshare, gshare),
        keep_gate + got[0].astype(F32),
        keep_up + got[1].astype(F32),
        keep_down,
    )


def local(*arrays, ndp):
    rows, heads = arrays[4].shape
    shard = arrays[11].shape[0]
    if ndp % 4 == 0 and rows % 8 == 0 and shard % 8 == 0 and heads * rows <= 128:
        return planes(*arrays, ndp=ndp)
    return whole_gather(*arrays)


def solution(mesh):
    in_specs = (
        P("dp", None),
        P("dp"),
        P("dp"),
        P("dp", "tensor", None),
        P("dp", "tensor"),
        P("dp", "tensor", None),
        P(None, "tensor"),
        P("dp", "tensor", None),
        P("dp", "tensor"),
        P("dp", "tensor", None),
        P("dp"),
        P(("dp", "tensor"), None),
        P(("dp", "tensor"), None),
        P(("dp", "tensor"), None),
        P("dp", None),
    )
    out_specs = (
        P("dp", None),
        P("dp", None),
        P("dp"),
        P("dp", "tensor", None),
        P("dp", "tensor"),
        P("dp", "tensor", None),
        P(None, "tensor"),
        P("dp", "tensor", None),
        P("dp", "tensor"),
        P("dp", "tensor", None),
        P("dp"),
        P(("dp", "tensor"), None),
        P(("dp", "tensor"), None),
        P(("dp", "tensor"), None),
    )
    return jax.shard_map(functools.partial(local, ndp=mesh.shape["dp"]), mesh=mesh, in_specs=in_specs, out_specs=out_specs, check_vma=False)
```

```python
import functools

import jax
import jax.numpy as jnp
import numpy as np
from jax import lax
from jax.experimental import pallas as pl
from jax.experimental.pallas import tpu as pltpu
from jax.sharding import PartitionSpec as P

EPS = 1e-06
ROPE_BASE = 1000000.0
NEG_BIG = -1e30


def rotate(field, flip_sign):
    half_dim = field.shape[-1] // 2
    places = jnp.arange(field.shape[0], dtype=jnp.float32)
    freqs = ROPE_BASE ** (-(jnp.arange(half_dim, dtype=jnp.float32) * 2.0 / field.shape[-1]))
    angles = places[:, None] * freqs[None, :]
    cosine = jnp.cos(angles)[:, None, :]
    sine = flip_sign * jnp.sin(angles)[:, None, :]
    first = field[..., :half_dim]
    second = field[..., half_dim:]
    return jnp.concatenate(
        [first * cosine - second * sine, second * cosine + first * sine], axis=-1
    )


def normed(field, gain):
    return field * lax.rsqrt(jnp.mean(field * field, axis=-1, keepdims=True) + EPS) * gain


def whole_gather(
    tokens,
    prefix,
    g_attn,
    w_query,
    b_query,
    w_key,
    b_key,
    w_value,
    b_value,
    w_out,
    g_mlp,
    w_gate,
    w_up,
    w_down,
    cotangent,
):
    gain_one, query_w, query_b, key_w, value_w, value_b, out_w = (
        lax.all_gather(g_attn, "dp", axis=0, tiled=True),
        lax.all_gather(w_query, "dp", axis=0, tiled=True),
        lax.all_gather(b_query, "dp", axis=0, tiled=True),
        lax.all_gather(w_key, "dp", axis=0, tiled=True),
        lax.all_gather(w_value, "dp", axis=0, tiled=True),
        lax.all_gather(b_value, "dp", axis=0, tiled=True),
        lax.all_gather(w_out, "dp", axis=0, tiled=True),
    )
    tok_float = tokens.astype(jnp.float32)
    gain_in = gain_one.astype(jnp.float32)
    normed_in = normed(tok_float, gain_in).astype(jnp.bfloat16)
    query_pre = (
        jnp.einsum("sd,ehd->she", normed_in, query_w, preferred_element_type=jnp.float32)
        + query_b.astype(jnp.float32).T
    )
    key_pre = (
        jnp.einsum("sd,ehd->she", normed_in, key_w, preferred_element_type=jnp.float32)
        + b_key.astype(jnp.float32).T
    )
    value_pre = (
        jnp.einsum("sd,ehd->she", normed_in, value_w, preferred_element_type=jnp.float32)
        + value_b.astype(jnp.float32).T
    )
    seq_len, heads_local, head_dim = query_pre.shape
    kv_local = key_pre.shape[1]
    group_size = heads_local // kv_local
    score_scale = head_dim ** (-0.5)
    query_rot = (
        rotate(query_pre, 1.0).astype(jnp.bfloat16).reshape(seq_len, kv_local, group_size, head_dim)
    )
    key_rot = rotate(key_pre, 1.0).astype(jnp.bfloat16)
    value_low = value_pre.astype(jnp.bfloat16)
    row_index = lax.broadcasted_iota(jnp.int32, (seq_len, seq_len), 0)
    col_index = lax.broadcasted_iota(jnp.int32, (seq_len, seq_len), 1)
    allowed = (col_index <= row_index) | (col_index < prefix[0])

    def score_of():
        raw_scores = (
            jnp.einsum("skgd,tkd->kgst", query_rot, key_rot, preferred_element_type=jnp.float32)
            * score_scale
        )
        return jnp.where(allowed, raw_scores, NEG_BIG)

    scores = score_of()
    row_peak = jnp.max(scores, axis=-1, keepdims=True)
    shifted_exp = jnp.exp(scores - row_peak)
    row_total = jnp.sum(shifted_exp, axis=-1, keepdims=True)
    probs_low = (shifted_exp / row_total).astype(jnp.bfloat16)
    log_total = row_peak + jnp.log(row_total)
    attended = jnp.einsum(
        "kgst,tkd->skgd", probs_low, value_low, preferred_element_type=jnp.float32
    )
    attended_low = attended.reshape(seq_len, heads_local, head_dim).astype(jnp.bfloat16)
    attn_part = jnp.einsum("she,ehd->sd", attended_low, out_w, preferred_element_type=jnp.float32)
    middle = tok_float + lax.psum(attn_part, "tensor")
    gain_two, gate_w, up_w, down_w = (
        lax.all_gather(g_mlp, "dp", axis=0, tiled=True),
        lax.all_gather(w_gate, "dp", axis=0, tiled=True),
        lax.all_gather(w_up, "dp", axis=0, tiled=True),
        lax.all_gather(w_down, "dp", axis=0, tiled=True),
    )
    gain_mid = gain_two.astype(jnp.float32)
    normed_mid = normed(middle, gain_mid).astype(jnp.bfloat16)
    contract = (((1,), (1,)), ((), ()))
    rows_first = (((0,), (0,)), ((), ()))
    gate_val = lax.dot_general(normed_mid, gate_w, contract, preferred_element_type=jnp.float32)
    up_val = lax.dot_general(normed_mid, up_w, contract, preferred_element_type=jnp.float32)
    sigmoid_gate = jax.nn.sigmoid(gate_val)
    silu_gate = gate_val * sigmoid_gate
    hidden = (silu_gate * up_val).astype(jnp.bfloat16)
    mlp_part = jnp.dot(hidden, down_w, preferred_element_type=jnp.float32)
    result = middle + lax.psum(mlp_part.astype(jnp.bfloat16), "tensor").astype(jnp.float32)
    out_tokens = result.astype(jnp.bfloat16)
    gain_two, gate_w, up_w, down_w = (
        lax.all_gather(g_mlp, "dp", axis=0, tiled=True),
        lax.all_gather(w_gate, "dp", axis=0, tiled=True),
        lax.all_gather(w_up, "dp", axis=0, tiled=True),
        lax.all_gather(w_down, "dp", axis=0, tiled=True),
    )
    cot_float = cotangent.astype(jnp.float32)
    grad_wdown = lax.dot_general(hidden, cotangent, rows_first, preferred_element_type=jnp.float32)
    grad_hidden = lax.dot_general(cotangent, down_w, contract, preferred_element_type=jnp.float32)
    grad_gate = (
        grad_hidden * up_val * sigmoid_gate * (1.0 + gate_val * (1.0 - sigmoid_gate))
    ).astype(jnp.bfloat16)
    grad_up = (grad_hidden * silu_gate).astype(jnp.bfloat16)
    grad_wgate = lax.dot_general(
        grad_gate, normed_mid, rows_first, preferred_element_type=jnp.float32
    )
    grad_wup = lax.dot_general(grad_up, normed_mid, rows_first, preferred_element_type=jnp.float32)
    mid_part = jnp.dot(grad_gate, gate_w, preferred_element_type=jnp.float32) + jnp.dot(
        grad_up, up_w, preferred_element_type=jnp.float32
    )
    grad_normed_mid = lax.psum(mid_part, "tensor")
    unused_mid, pull_mid = jax.vjp(normed, middle, gain_mid)
    grad_mid_norm, grad_gmlp = pull_mid(grad_normed_mid)
    grad_middle = cot_float + grad_mid_norm
    gain_one, query_w, query_b, key_w, value_w, value_b, out_w = (
        lax.all_gather(g_attn, "dp", axis=0, tiled=True),
        lax.all_gather(w_query, "dp", axis=0, tiled=True),
        lax.all_gather(b_query, "dp", axis=0, tiled=True),
        lax.all_gather(w_key, "dp", axis=0, tiled=True),
        lax.all_gather(w_value, "dp", axis=0, tiled=True),
        lax.all_gather(b_value, "dp", axis=0, tiled=True),
        lax.all_gather(w_out, "dp", axis=0, tiled=True),
    )
    middle_low = grad_middle.astype(jnp.bfloat16)
    grad_wout = jnp.einsum(
        "she,sd->ehd", attended_low, middle_low, preferred_element_type=jnp.float32
    )
    grad_attended = (
        jnp.einsum("sd,ehd->she", middle_low, out_w, preferred_element_type=jnp.float32)
        .astype(jnp.bfloat16)
        .reshape(seq_len, kv_local, group_size, head_dim)
    )
    probs_again = jnp.exp(score_of() - log_total)
    again_low = probs_again.astype(jnp.bfloat16)
    grad_value = jnp.einsum(
        "kgst,skgd->tkd", again_low, grad_attended, preferred_element_type=jnp.float32
    ).astype(jnp.bfloat16)
    grad_probs = jnp.einsum(
        "skgd,tkd->kgst", grad_attended, value_low, preferred_element_type=jnp.float32
    )
    inner_sum = jnp.sum(probs_again * grad_probs, axis=-1, keepdims=True)
    grad_scores = (probs_again * (grad_probs - inner_sum)).astype(jnp.bfloat16)
    grad_qrot = (
        jnp.einsum(
            "kgst,tkd->skgd", grad_scores, key_rot, preferred_element_type=jnp.float32
        ).reshape(seq_len, heads_local, head_dim)
        * score_scale
    )
    grad_krot = (
        jnp.einsum("kgst,skgd->tkd", grad_scores, query_rot, preferred_element_type=jnp.float32)
        * score_scale
    )
    grad_query = rotate(grad_qrot, -1.0).astype(jnp.bfloat16)
    grad_key = rotate(grad_krot, -1.0).astype(jnp.bfloat16)
    grad_wquery = jnp.einsum(
        "she,sd->ehd", grad_query, normed_in, preferred_element_type=jnp.float32
    )
    grad_bquery = jnp.sum(grad_query.astype(jnp.float32), axis=0).T
    grad_wkey = jnp.einsum("she,sd->ehd", grad_key, normed_in, preferred_element_type=jnp.float32)
    grad_bkey = jnp.sum(grad_key.astype(jnp.float32), axis=0).T
    key_bias_total = lax.psum(grad_bkey, "dp")
    grad_wvalue = jnp.einsum(
        "she,sd->ehd", grad_value, normed_in, preferred_element_type=jnp.float32
    )
    grad_bvalue = jnp.sum(grad_value.astype(jnp.float32), axis=0).T
    in_part = jnp.einsum("she,ehd->sd", grad_query, query_w, preferred_element_type=jnp.float32)
    in_part = in_part + jnp.einsum(
        "she,ehd->sd", grad_key, key_w, preferred_element_type=jnp.float32
    )
    in_part = in_part + jnp.einsum(
        "she,ehd->sd", grad_value, value_w, preferred_element_type=jnp.float32
    )
    grad_normed_in = lax.psum(in_part.astype(jnp.bfloat16), "tensor").astype(jnp.float32)
    unused_in, pull_in = jax.vjp(normed, tok_float, gain_in)
    grad_in_norm, grad_gattn = pull_in(grad_normed_in)
    grad_tokens = grad_middle + grad_in_norm
    every_sum = (
        lax.psum_scatter(grad_gattn, "dp", scatter_dimension=0, tiled=True),
        lax.psum_scatter(grad_wquery, "dp", scatter_dimension=0, tiled=True),
        lax.psum_scatter(grad_bquery, "dp", scatter_dimension=0, tiled=True),
        lax.psum_scatter(grad_wkey, "dp", scatter_dimension=0, tiled=True),
        lax.psum_scatter(grad_wvalue, "dp", scatter_dimension=0, tiled=True),
        lax.psum_scatter(grad_bvalue, "dp", scatter_dimension=0, tiled=True),
        lax.psum_scatter(grad_wout, "dp", scatter_dimension=0, tiled=True),
        lax.psum_scatter(grad_gmlp, "dp", scatter_dimension=0, tiled=True),
        lax.psum_scatter(grad_wgate, "dp", scatter_dimension=0, tiled=True),
        lax.psum_scatter(grad_wup, "dp", scatter_dimension=0, tiled=True),
        lax.psum_scatter(grad_wdown, "dp", scatter_dimension=0, tiled=True),
    )
    attn_grads = every_sum[:7]
    mlp_grads = every_sum[7:]
    return (
        out_tokens,
        grad_tokens,
        attn_grads[0],
        attn_grads[1],
        attn_grads[2],
        attn_grads[3],
        key_bias_total,
        attn_grads[4],
        attn_grads[5],
        attn_grads[6],
        mlp_grads[0],
        mlp_grads[1],
        mlp_grads[2],
        mlp_grads[3],
    )


MESH = pl.DeviceIdType.MESH
BF = jnp.bfloat16
F32 = jnp.float32
NT = (((1,), (1,)), ((), ()))
NN = (((1,), (0,)), ((), ()))
TN = (((0,), (0,)), ((), ()))
VMEM_LIMIT = 67043328
ANY = pl.BlockSpec(memory_space=pl.ANY)
VM = pl.BlockSpec(memory_space=pltpu.VMEM)


def dot(a, b, dims):
    return lax.dot_general(a, b, dims, preferred_element_type=F32)


class Spot:
    def __init__(self, nz):
        self.nz = nz
        self.dp = lax.axis_index("dp")
        self.t = lax.axis_index("tensor")
        self.z, self.x, self.c = self.dp // 4, (self.dp // 2) % 2, self.dp % 2
        self.xn = (self.index(self.z, 1 - self.x, self.c), self.t)
        self.cn = (self.index(self.z, self.x, 1 - self.c), self.t)
        self.yn = (self.dp, 1 - self.t)

    def index(self, z, x, c):
        return (z * 2 + x) * 2 + c

    def near(self, k):
        nz, z = self.nz, self.z
        edge = jnp.minimum(z, nz - 1 - z)
        side = jnp.where(z <= nz - 1 - z, -1, 1)
        half = (k + 1) // 2
        close = side * half if k % 2 else -side * half
        return z + jnp.where(k <= 2 * edge, close, -side * (k - edge))

    def line(self, k):
        return (self.index(self.near(k), self.x, self.c), self.t)

    def step(self, way):
        z = jnp.clip(self.z + way, 0, self.nz - 1)
        return (self.index(z, self.x, self.c), self.t)


class Wires:
    def __init__(self):
        self.sent = []

    def send(self, src, dst, send_sem, recv_sem, device, only=None):
        copy = pltpu.make_async_remote_copy(
            src_ref=src,
            dst_ref=dst,
            send_sem=send_sem,
            recv_sem=recv_sem,
            device_id=device,
            device_id_type=MESH,
        )
        if only is None:
            copy.start()
        else:
            pl.when(only)(copy.start)
        self.sent.append((copy, only))

    def landed(self, dst, recv_sem, spot):
        pltpu.make_async_remote_copy(
            src_ref=dst,
            dst_ref=dst,
            send_sem=recv_sem,
            recv_sem=recv_sem,
            device_id=spot.xn,
            device_id_type=MESH,
        ).wait_recv()

    def drain(self):
        for copy, only in self.sent:
            if only is None:
                copy.wait_send()
            else:
                pl.when(only)(copy.wait_send)
        self.sent = []


class Gather:
    def __init__(self, at, wires, slot, recv, send, core=None):
        self.at, self.wires, self.slot, self.recv, self.send, self.core = at, wires, slot, recv, send, core

    def hand(self, src, z, x, lane, device, only=None):
        self.wires.send(src, self.slot(z, x), self.send.at[lane], self.recv.at[z, x], device, only)

    def to_core(self, src, z, x, lane, only=None):
        if self.core is not None:
            slot, recv, send = self.core
            self.wires.send(src, slot(z, x), send.at[lane], recv.at[z, x], self.at.cn, only)

    def start(self, src):
        at = self.at
        self.hand(src, at.z, at.x, 0, at.step(1), at.z < at.nz - 1)
        self.hand(src, at.z, at.x, 1, at.step(-1), at.z > 0)
        self.hand(src, at.z, at.x, 2, at.xn)
        self.to_core(src, at.z, at.x, 0)

    def relay(self, k):
        at = self.at
        for side, way in ((0, 1), (1, -1)):
            z = at.z - way * k
            real = (z >= 0) & (z < at.nz)
            block = self.slot(z, at.x)
            pl.when(real)(functools.partial(self.wires.landed, block, self.recv.at[z, at.x], at))
            lane = 3 * k + side * 3 * (at.nz - 1)
            ahead = at.z + way
            self.hand(block, z, at.x, lane, at.step(way), real & (ahead >= 0) & (ahead < at.nz))
            self.hand(block, z, at.x, lane + 1, at.xn, real)
            self.to_core(block, z, at.x, k + side * (at.nz - 1), real)

    def column(self, k):
        at = self.at
        z = at.near(k)
        block = self.slot(z, 1 - at.x)
        self.wires.landed(block, self.recv.at[z, 1 - at.x], at)
        self.to_core(block, z, 1 - at.x, 2 * at.nz - 1 + k)

    @staticmethod
    def lanes(nz):
        return 3 + 6 * (nz - 1)

    @staticmethod
    def core_lanes(nz):
        return 3 * nz - 1


class LineSum:
    def __init__(self, at, wires, inbox, outbox, recv, send):
        self.at, self.wires, self.inbox, self.outbox, self.recv, self.send = at, wires, inbox, outbox, recv, send

    def push(self, k, acc_ref):
        self.outbox[k] = acc_ref[...].astype(BF)
        self.pass_on(k, self.outbox.at[k])

    def pass_on(self, k, ref):
        at = self.at
        self.wires.send(ref, self.inbox.at[at.z], self.send.at[k], self.recv.at[at.z], at.line(k))

    def close(self, acc_ref):
        at = self.at
        for k in range(1, at.nz):
            z = at.near(k)
            self.wires.landed(self.inbox.at[z], self.recv.at[z], at)
            acc_ref[...] += self.inbox[z].astype(F32)


class OwnerSum:
    def __init__(self, at, wires, full, rows, bufs, sems):
        self.at, self.wires, self.full, self.rows = at, wires, full, rows
        self.core_out, self.core_in, self.x_out, self.x_in, outbox, inbox, self.acc = bufs
        self.a_recv, self.a_send, self.x_recv, self.x_send, z_recv, z_send = sems
        self.line = LineSum(at, wires, inbox, outbox, z_recv, z_send)
        self.order = list(range(at.nz - 1, -1, -1))

    @staticmethod
    def buffers(nz, units, rows, wide):
        block = (units * rows, wide)
        vm = pltpu.VMEM
        return [
            vm((nz, 2) + block, BF),
            vm((nz, 2) + block, BF),
            vm((nz,) + block, BF),
            vm((nz,) + block, BF),
            vm((nz,) + block, BF),
            vm((nz,) + block, BF),
            vm(block, F32),
        ]

    @staticmethod
    def semaphores(nz):
        dma = pltpu.SemaphoreType.DMA
        return [dma((nz, 2)), dma((nz, 2)), dma((nz,)), dma((nz,)), dma((nz,)), dma((nz,))]

    def terms(self, z, x, c):
        start = pl.multiple_of(self.at.index(z, x, c) * self.rows, self.rows)
        piece = self.full[:, pl.ds(start, self.rows), :]
        return piece.reshape(piece.shape[0] * self.rows, piece.shape[2])

    def to_core(self):
        at = self.at
        for far in (1, 0):
            for k in self.order:
                x = 1 - at.x if far else at.x
                self.core_out[k, far] = self.terms(at.near(k), x, 1 - at.c).astype(BF)
                self.wires.send(
                    self.core_out.at[k, far],
                    self.core_in.at[k, far],
                    self.a_send.at[k, far],
                    self.a_recv.at[k, far],
                    at.cn,
                )

    def across(self):
        at = self.at
        for k in self.order:
            self.wires.landed(self.core_in.at[k, 1], self.a_recv.at[k, 1], at)
            both = self.terms(at.near(k), 1 - at.x, at.c) + self.core_in[k, 1].astype(F32)
            self.x_out[k] = both.astype(BF)
            self.wires.send(self.x_out.at[k], self.x_in.at[k], self.x_send.at[k], self.x_recv.at[k], at.xn)

    def along(self, out):
        at = self.at
        for k in self.order:
            self.wires.landed(self.core_in.at[k, 0], self.a_recv.at[k, 0], at)
            self.wires.landed(self.x_in.at[k], self.x_recv.at[k], at)
            acc = self.acc if k else out
            acc[...] = (
                self.terms(at.near(k), at.x, at.c)
                + self.core_in[k, 0].astype(F32)
                + self.x_in[k].astype(F32)
            )
            if k:
                self.line.push(k, acc)

    def close(self, out):
        self.line.close(out)


def greet(devices):
    barrier = pltpu.get_barrier_semaphore()
    for device in devices:
        pl.semaphore_signal(barrier, inc=1, device_id=device, device_id_type=MESH)
    pl.semaphore_wait(barrier, len(devices))


def turn(field, cos, sin):
    return field * cos + pltpu.roll(field, field.shape[-1] // 2, 1) * sin


def attn_kernel(
    nz,
    scale,
    tok_in,
    prefix_in,
    key_b_in,
    cos_in,
    sin_in,
    qkv_in,
    wo_in,
    small_in,
    cot_in,
    gate_in,
    up_in,
    down_in,
    att,
    q_rot,
    kv,
    probs,
    nm_in,
    gains,
    nm_half,
    mid_half,
    qkv,
    wo,
    cot,
    mlp_w,
    stage_a,
    stage_b,
    small,
    qkv_w,
    out_w,
    part,
    y_out,
    y_in,
    local_sem,
    q_recv,
    q_send,
    q_core_recv,
    q_core_send,
    o_recv,
    o_send,
    o_core_recv,
    o_core_send,
    s_recv,
    s_send,
    c_recv,
    c_send,
    w_recv,
    w_send,
    y_recv,
    y_send,
):
    at = Spot(nz)
    ndp = 4 * nz
    half, wide = mid_half.shape
    seq = 2 * half
    units, head_dim = qkv_w.shape[:2]
    heads = units - 2
    rows = qkv_in.shape[1]
    others = [(lax.rem(at.dp + p, ndp), at.t) for p in range(1, ndp)]

    def load(src, dst, i):
        copy = pltpu.make_async_copy(src, dst, local_sem.at[i])
        copy.start()
        return copy

    staged = [load(qkv_in, stage_a, 0), load(wo_in, stage_b, 1), load(small_in, small.at[at.dp], 2)]
    greet(others + [at.yn])
    wires = Wires()

    def part_of(ref, core):
        def slot(z, x):
            owner = at.index(z, x, core)
            return ref.at[:, pl.ds(pl.multiple_of(owner * rows, rows), rows), :]

        return slot

    def cot_slot(z, x):
        return cot.at[z, x]

    q_slot, o_slot = part_of(qkv, at.c), part_of(wo, at.c)
    gq = Gather(at, wires, q_slot, q_recv, q_send, (q_slot, q_core_recv, q_core_send))
    go = Gather(at, wires, o_slot, o_recv, o_send, (o_slot, o_core_recv, o_core_send))
    gc = Gather(at, wires, cot_slot, c_recv, c_send)
    mine = at.c * 2 + at.t
    across = at.c * 2 + 1 - at.t

    def give_weight(i, src):
        wires.send(src, mlp_w.at[i, mine], w_send.at[0, i], w_recv.at[i, mine], at.yn)

    shard = down_in.shape[0]
    early = shard * 2 // 7 // 16 * 16
    pieces = (pl.ds(0, early), pl.ds(early, shard - early))

    def give_down(n):
        dst = mlp_w.at[2, mine, pieces[n]]
        wires.send(down_in.at[pieces[n]], dst, w_send.at[0, 2 + n], w_recv.at[2 + n, mine], at.yn)

    for n, device in enumerate(others):
        wires.send(small_in, small.at[at.dp], s_send.at[n], s_recv.at[at.dp], device)
    gq.start(qkv_in)
    give_weight(0, gate_in)
    give_weight(1, up_in)
    give_down(0)
    go.start(wo_in)
    for i, src in enumerate((gate_in, up_in, down_in)):
        wires.send(src, mlp_w.at[i, mine], w_send.at[1, i], w_recv.at[i, mine], at.cn)
    for copy in staged:
        copy.wait()
    placed = [load(stage_a, q_slot(at.z, at.x), 3), load(stage_b, o_slot(at.z, at.x), 4)]

    for device in others:
        wires.landed(small.at[device[0]], s_recv.at[device[0]], at)
    lanes = small.shape[2]
    share = wide // ndp
    spread = jnp.zeros((small.shape[1], wide), F32)
    bias = jnp.zeros((8, lanes), F32)
    blank = jnp.zeros((small.shape[1], wide - lanes), F32)
    for d in range(ndp):
        tile = small[d].astype(F32)
        row = jnp.concatenate([tile, blank], axis=1)
        spread = spread + (pltpu.roll(row, d * share, 1) if d else row)
        bias = bias + (pltpu.roll(tile[:8], d * rows, 1) if d else tile[:8])
    gains[0:1] = spread[0:1]
    gains[1:2] = spread[8:9]

    gq.relay(1)
    tok = tok_in[...].astype(F32)
    rms = lax.rsqrt(jnp.mean(tok * tok, axis=-1, keepdims=True) + EPS)
    nm_in[...] = (tok * rms * spread[0:1]).astype(BF)
    go.relay(1)
    for k in range(2, nz):
        gq.relay(k)
        go.relay(k)
    gc.start(cot_in.at[pl.ds(pl.multiple_of(at.t * half, half), half), :])
    for k in range(nz):
        gq.column(k)

    def core_blocks(ref, recv):
        slot = part_of(ref, 1 - at.c)
        for z in range(nz):
            for x in range(2):
                wires.landed(slot(z, x), recv.at[z, x], at)

    core_blocks(qkv, q_core_recv)
    for copy in placed:
        copy.wait()
    load(qkv, qkv_w, 5).wait()
    cos, sin = cos_in[...], sin_in[...]
    pair = 2 * head_dim
    for u in range(0, units, 2):
        pre = dot(nm_in[...], qkv_w[u : u + 2].reshape(pair, wide), NT)
        for v in range(2):
            field = pre[:, v * head_dim : (v + 1) * head_dim]
            if u + v < heads:
                q_rot[u + v] = turn(field + bias[1 + u + v : 2 + u + v], cos, sin).astype(BF)
            elif u + v == heads:
                kv[0] = turn(field + key_b_in[...], cos, sin).astype(BF)
            else:
                kv[1] = (field + bias[1 + heads : 2 + heads]).astype(BF)
    for k in range(nz):
        go.column(k)
    scores = (dot(q_rot[...].reshape(heads * seq, head_dim), kv[0], NT) * scale).reshape(heads, seq, seq)
    row_index = lax.broadcasted_iota(jnp.int32, (seq, seq), 0)
    col_index = lax.broadcasted_iota(jnp.int32, (seq, seq), 1)
    allowed = (col_index <= row_index) | (col_index < prefix_in[0])
    scores = jnp.where(allowed[None], scores, NEG_BIG)
    shifted = jnp.exp(scores - jnp.max(scores, axis=-1, keepdims=True))
    probs[...] = shifted / jnp.sum(shifted, axis=-1, keepdims=True)
    mixed = dot(probs[...].reshape(heads * seq, seq).astype(BF), kv[1], NN).astype(BF)
    for h in range(heads):
        att[:, h * head_dim : (h + 1) * head_dim] = mixed[h * seq : (h + 1) * seq]
    core_blocks(wo, o_core_recv)
    load(wo, out_w, 6).wait()
    part[...] = dot(att[...], out_w[...].reshape(heads * head_dim, wide), NN)
    far_row = pl.multiple_of((1 - at.t) * half, half)
    own_row = pl.multiple_of(at.t * half, half)
    y_out[...] = part[pl.ds(far_row, half), :].astype(BF)
    wires.send(y_out, y_in, y_send.at[0], y_recv.at[0], at.yn)
    give_down(1)
    for k in range(1, nz - 1):
        gc.relay(k)
    wires.landed(y_in, y_recv.at[0], at)
    middle = (
        tok_in[pl.ds(own_row, half), :].astype(F32) + part[pl.ds(own_row, half), :] + y_in[...].astype(F32)
    )
    rms = lax.rsqrt(jnp.mean(middle * middle, axis=-1, keepdims=True) + EPS)
    mid_half[...] = middle
    nm_half[...] = (middle * rms * gains[1:2]).astype(BF)
    gc.relay(nz - 1)
    for k in range(nz):
        gc.column(k)
    arrivals = [(mlp_w.at[i, across], i) for i in range(2)]
    arrivals += [(mlp_w.at[2, across, pieces[n]], 2 + n) for n in range(2)]
    for ref, i in arrivals:
        wires.landed(ref, w_recv.at[i, across], at)
        wires.send(ref, ref, w_send.at[2, i], w_recv.at[i, across], at.cn)
    there = (1 - at.c) * 2
    for i in range(3):
        wires.landed(mlp_w.at[i, there + at.t], w_recv.at[i, there + at.t], at)
    there = there + 1 - at.t
    for i in range(2):
        wires.landed(mlp_w.at[i, there], w_recv.at[i, there], at)
    for n in range(2):
        wires.landed(mlp_w.at[2, there, pieces[n]], w_recv.at[2 + n, there], at)
    wires.drain()


def attn_step(nz, scale, tokens, prefix, key_b, cos, sin, qkv, wo, small, cotangent, gate, up, down):
    ndp = 4 * nz
    seq, wide = tokens.shape
    half = seq // 2
    units, rows = qkv.shape[:2]
    heads, head_dim = units - 2, ndp * rows
    shape = jax.ShapeDtypeStruct
    dma = pltpu.SemaphoreType.DMA
    vm = pltpu.VMEM
    return pl.pallas_call(
        functools.partial(attn_kernel, nz, scale),
        out_shape=(
            shape((seq, heads * head_dim), BF),
            shape((heads, seq, head_dim), BF),
            shape((2, seq, head_dim), BF),
            shape((heads, seq, seq), F32),
            shape((seq, wide), BF),
            shape((2, wide), F32),
            shape((half, wide), BF),
            shape((half, wide), F32),
            shape((units, head_dim, wide), BF),
            shape((heads, head_dim, wide), BF),
            shape((nz, 2, half, wide), BF),
            shape((3, 4) + gate.shape, BF),
        ),
        in_specs=[VM, pl.BlockSpec(memory_space=pltpu.SMEM), VM, VM, VM] + [ANY] * 7,
        out_specs=[VM] * 8 + [ANY] * 4,
        scratch_shapes=[
            vm(qkv.shape, BF),
            vm(wo.shape, BF),
            vm((ndp,) + small.shape, BF),
            vm((units, head_dim, wide), BF),
            vm((heads, head_dim, wide), BF),
            vm((seq, wide), F32),
            vm((half, wide), BF),
            vm((half, wide), BF),
            dma((7,)),
            dma((nz, 2)),
            dma((Gather.lanes(nz),)),
            dma((nz, 2)),
            dma((Gather.core_lanes(nz),)),
            dma((nz, 2)),
            dma((Gather.lanes(nz),)),
            dma((nz, 2)),
            dma((Gather.core_lanes(nz),)),
            dma((ndp,)),
            dma((ndp,)),
            dma((nz, 2)),
            dma((Gather.lanes(nz),)),
            dma((4, 4)),
            dma((3, 4)),
            dma((1,)),
            dma((1,)),
        ],
        compiler_params=pltpu.CompilerParams(
            collective_id=1, has_side_effects=True, vmem_limit_bytes=VMEM_LIMIT
        ),
        name="attn_step",
    )(tokens, prefix, key_b, cos, sin, qkv, wo, small, cotangent, gate, up, down)


def mlp_kernel(
    nz,
    nm_in,
    mid_half,
    gains,
    cot_in,
    mlp_in,
    cot_own_in,
    gate_in,
    up_in,
    down_in,
    out_cols,
    out_near,
    keep_gate,
    keep_up,
    keep_down,
    give,
    grad_half,
    gain_send,
    weights,
    cot,
    nm,
    gh,
    hid,
    gg,
    gu,
    own,
    xs,
    xr,
    z_in,
    pair,
    grads,
    partner,
    down_send,
    down_recv,
    o_out,
    o_in,
    local_sem,
    n_recv,
    n_send,
    x_recv,
    x_send,
    z_recv,
    z_send,
    p_recv,
    p_send,
    o_recv,
    o_send,
    y_recv,
    y_send,
):
    at = Spot(nz)
    half, wide = nm.shape[2], nm.shape[3]
    two = 2 * half
    shard = mlp_in.shape[2]
    padded = weights.shape[2]
    units = 4 * padded
    wires = Wires()
    mine = at.c * 2 + at.t

    loads = []

    def load(src, dst, sem):
        copy = pltpu.make_async_copy(src, dst, sem)
        copy.start()
        loads.append(copy)
        return copy

    per = [[], [], []]
    for i, src in ((2, down_in), (0, gate_in), (1, up_in)):
        per[i].append(load(src, weights.at[i, mine, pl.ds(0, shard)], local_sem.at[i * 4]))
        for j, slot in enumerate((at.c * 2 + 1 - at.t, (1 - at.c) * 2, (1 - at.c) * 2 + 1)):
            per[i].append(
                load(mlp_in.at[i, slot], weights.at[i, slot, pl.ds(0, shard)], local_sem.at[i * 4 + 1 + j])
            )
    cot_loads = [
        load(
            cot_own_in.at[pl.ds(pl.multiple_of(at.t * half, half), half), :],
            cot.at[at.z, at.x],
            local_sem.at[12],
        )
    ]
    for k in range(nz):
        zk = at.near(k)
        if k:
            cot_loads.append(load(cot_in.at[zk, at.x], cot.at[zk, at.x], local_sem.at[12 + 2 * k]))
        cot_loads.append(load(cot_in.at[zk, 1 - at.x], cot.at[zk, 1 - at.x], local_sem.at[13 + 2 * k]))
    for i in range(3):
        for s in range(4):
            weights[i, s, shard:padded, :] = jnp.zeros((padded - shard, wide), BF)

    loaded_nm = load(nm_in, nm.at[at.z, at.x], local_sem.at[12 + 2 * nz])
    greet([at.xn, at.yn, at.cn] + [at.line(k) for k in range(1, nz)])

    def nm_slot(z, x):
        return nm.at[z, x]

    gather = Gather(at, wires, nm_slot, n_recv, n_send)
    line = LineSum(at, wires, z_in, xr, z_recv, z_send)
    gather.start(nm_in)
    gain = gains[1:2]
    gate_w, up_w, down_w = weights.at[0], weights.at[1], weights.at[2]
    for copy in per[2] + cot_loads:
        copy.wait()

    def hidden_grad(z, carry):
        gh[z] = dot(cot[z].reshape(two, wide), down_w[...].reshape(units, wide), NT)
        return carry

    lax.fori_loop(0, nz - 1, hidden_grad, 0)
    gather.relay(1)
    hidden_grad(nz - 1, 0)
    for copy in per[0] + per[1] + [loaded_nm]:
        copy.wait()

    def hand_over(k):
        wires.send(xs.at[k], xr.at[k], x_send.at[k], x_recv.at[k], at.xn)

    def column_sum(k):
        wires.landed(xr.at[k], x_recv.at[k], at)
        own[k] += xr[k].astype(F32)
        if k:
            line.push(k, own.at[k])

    for k in range(nz):
        zk = at.near(k)
        gather.column(k)
        a = nm[zk].reshape(two, wide)
        gate = dot(a, gate_w[...].reshape(units, wide), NT)
        up = dot(a, up_w[...].reshape(units, wide), NT)
        sig = jax.nn.sigmoid(gate)
        silu = gate * sig
        hid[zk] = (silu * up).astype(BF)
        ghk = gh[zk]
        gg[zk] = (ghk * up * sig * (1.0 + gate * (1.0 - sig))).astype(BF)
        gu[zk] = (ghk * silu).astype(BF)
        if k + 2 < nz:
            gather.relay(k + 2)
        pair[...] = (
            dot(gg[zk], gate_w[...].reshape(units, wide), NN)
            + dot(gu[zk], up_w[...].reshape(units, wide), NN)
        ).reshape(2, half, wide)
        xs[k] = pair[1 - at.x].astype(BF)
        own[k] = pair[at.x]
        if k:
            hand_over(k)
        if k > 1:
            column_sum(k - 1)
    hand_over(0)
    tile = 512

    def weight_grad(i, lhs, rhs):
        def columns(j, carry):
            cols = pl.ds(pl.multiple_of(j * tile, tile), tile)
            right = rhs[:, :, :, cols].reshape(nz * two, tile)
            acc = dot(lhs[...].reshape(nz * two, units), right, TN).astype(BF).reshape(4, padded, tile)
            grads[i, :, :, cols] = acc[:, :shard]
            return carry

        lax.fori_loop(0, wide // tile, columns, 0)
        for j in range(2):
            wires.send(
                grads.at[i, (1 - at.c) * 2 + j], partner.at[i, j], p_send.at[i, j], p_recv.at[i, j], at.cn
            )

    def chip_sum(i, kept, given):
        for j in range(2):
            wires.landed(partner.at[i, j], p_recv.at[i, j], at)
        kept[...] = grads[i, mine].astype(F32) + partner[i, at.t].astype(F32)
        given[...] = (
            grads[i, at.c * 2 + 1 - at.t].astype(F32) + partner[i, 1 - at.t].astype(F32)
        ).astype(BF)

    weight_grad(2, hid, cot)
    column_sum(nz - 1)

    def mlp_out(z, carry):
        pair[...] = dot(hid[z], down_w[...].reshape(units, wide), NN).reshape(2, half, wide)
        o_out[z] = pair[1 - at.x].astype(BF)
        out_cols[z] = pair[at.x].astype(BF)
        return carry

    lax.fori_loop(0, nz, mlp_out, 0)
    for k in range(nz - 1, 0, -1):
        wires.send(o_out.at[at.near(k)], o_in.at[k], o_send.at[k], o_recv.at[k], at.xn)
    out_near[...] = o_out[at.z]
    chip_sum(2, keep_down, down_send)
    wires.send(down_send, down_recv, y_send.at[0], y_recv.at[0], at.yn)
    weight_grad(0, gg, nm)
    weight_grad(1, gu, nm)
    column_sum(0)
    line.close(own.at[0])
    total = own[0]
    middle = mid_half[...]
    rms = lax.rsqrt(jnp.mean(middle * middle, axis=-1, keepdims=True) + EPS)
    unit = middle * rms
    gain_send[...] = jnp.sum(total * unit, axis=0, keepdims=True)
    scaled = total * gain
    cot_f = cot[at.z, at.x].astype(F32)
    grad_mid = cot_f + rms * (scaled - unit * jnp.mean(scaled * unit, axis=-1, keepdims=True))
    grad_half[...] = grad_mid.astype(BF)
    chip_sum(0, keep_gate, give.at[0])
    chip_sum(1, keep_up, give.at[1])
    for k in range(nz - 1, 0, -1):
        wires.landed(o_in.at[k], o_recv.at[k], at)
        zk = at.near(k)
        out_cols[zk] = (out_cols[zk].astype(F32) + o_in[k].astype(F32)).astype(BF)
    wires.landed(down_recv, y_recv.at[0], at)
    keep_down[...] += down_recv[...].astype(F32)
    wires.drain()


def mlp_step(nz, nm_half, mid_half, gains, cot_all, mlp_all, cotangent, gate, up, down):
    half, wide = cotangent.shape[0] // 2, cotangent.shape[1]
    shard = gate.shape[0]
    padded = -(-shard // 32) * 32
    units = 4 * padded
    shape = jax.ShapeDtypeStruct
    dma = pltpu.SemaphoreType.DMA
    vm = pltpu.VMEM
    return pl.pallas_call(
        functools.partial(mlp_kernel, nz),
        out_shape=(
            shape((nz, half, wide), BF),
            shape((half, wide), BF),
            shape((shard, wide), F32),
            shape((shard, wide), F32),
            shape((shard, wide), F32),
            shape((2, shard, wide), BF),
            shape((half, wide), BF),
            shape((1, wide), F32),
        ),
        in_specs=[VM, VM, VM] + [ANY] * 6,
        out_specs=[VM] * 8,
        scratch_shapes=[
            vm((3, 4, padded, wide), BF),
            vm((nz, 2, half, wide), BF),
            vm((nz, 2, half, wide), BF),
            vm((nz, 2 * half, units), F32),
            vm((nz, 2 * half, units), BF),
            vm((nz, 2 * half, units), BF),
            vm((nz, 2 * half, units), BF),
            vm((nz, half, wide), F32),
            vm((nz, half, wide), BF),
            vm((nz, half, wide), BF),
            vm((nz, half, wide), BF),
            vm((2, half, wide), F32),
            vm((3, 4, shard, wide), BF),
            vm((3, 2, shard, wide), BF),
            vm((shard, wide), BF),
            vm((shard, wide), BF),
            vm((nz, half, wide), BF),
            vm((nz, half, wide), BF),
            dma((12 + 2 * nz + 1,)),
            dma((nz, 2)),
            dma((Gather.lanes(nz),)),
            dma((nz,)),
            dma((nz,)),
            dma((nz,)),
            dma((nz,)),
            dma((3, 2)),
            dma((3, 2)),
            dma((nz,)),
            dma((nz,)),
            dma((1,)),
            dma((1,)),
        ],
        compiler_params=pltpu.CompilerParams(
            collective_id=2, has_side_effects=True, vmem_limit_bytes=VMEM_LIMIT
        ),
        name="mlp_step",
    )(nm_half, mid_half, gains, cot_all, mlp_all, cotangent, gate, up, down)


def tail_kernel(
    nz,
    scale,
    out_cols,
    out_near,
    mid_half,
    grad_half,
    gain_part,
    att,
    q_rot,
    kv,
    probs,
    nm_in,
    tok_in,
    gain_in,
    cos_in,
    sin_in,
    qkv_in,
    wo_in,
    give,
    gq,
    go,
    out_tokens,
    grad_tokens,
    small,
    got,
    mid_low,
    gain_got,
    qkv_w,
    out_w,
    full_q,
    full_o,
    ga,
    gs,
    gpre,
    in_part,
    in_got,
    b_x,
    b_in,
    b_acc,
    out_send,
    out_got,
    small_all,
    local_sem,
    b_xrecv,
    b_xsend,
    b_zrecv,
    b_zsend,
    y_recv,
    y_send,
    s_recv,
    s_send,
    *owner_refs,
):
    at = Spot(nz)
    ndp = 4 * nz
    half, wide = mid_half.shape
    seq = 2 * half
    heads, head_dim = full_o.shape[:2]
    rows = head_dim // ndp
    others = [(lax.rem(at.dp + p, ndp), at.t) for p in range(1, ndp)]
    loads = [
        pltpu.make_async_copy(wo_in, out_w, local_sem.at[0]),
        pltpu.make_async_copy(qkv_in, qkv_w, local_sem.at[1]),
    ]
    for load in loads:
        load.start()
    greet(others + [at.yn])
    wires = Wires()
    sum_q = OwnerSum(at, wires, full_q, rows, owner_refs[:7], owner_refs[14:20])
    sum_o = OwnerSum(at, wires, full_o, rows, owner_refs[7:14], owner_refs[20:26])
    out_line = LineSum(at, wires, b_in, None, b_zrecv, b_zsend)

    def swap_y(i, src, dst):
        wires.send(src, dst, y_send.at[i], y_recv.at[i], at.yn)

    swap_y(0, grad_half, mid_low.at[at.t])
    swap_y(1, gain_part, gain_got)
    wires.send(out_near, b_x, b_xsend.at[0], b_xrecv.at[0], at.xn)
    for k in range(nz - 1, 0, -1):
        out_line.pass_on(k, out_cols.at[at.near(k)])
    mid_low[at.t] = grad_half[...]
    wires.landed(mid_low.at[1 - at.t], y_recv.at[0], at)
    swap_y(2, give.at[0], got.at[0])
    loads[0].wait()
    low = mid_low[...].reshape(seq, wide)
    att_grad = dot(low, out_w[...].reshape(heads * head_dim, wide), NT).astype(BF)
    for h in range(heads):
        ga[h] = att_grad[:, h * head_dim : (h + 1) * head_dim]
    tile = 512

    def weight_grad(full, lhs, rhs_of):
        for j in range(wide // tile):
            cols = slice(j * tile, (j + 1) * tile)
            full[:, :, cols] = dot(lhs, rhs_of(cols), TN).reshape(full.shape[0], head_dim, tile)

    weight_grad(full_o, att[...], lambda cols: mid_low[:, :, cols].reshape(seq, tile))
    sum_o.to_core()

    ga_all = ga[...].reshape(heads * seq, head_dim)
    p = probs[...].reshape(heads * seq, seq)
    key, value = kv[0], kv[1]
    grad_value = dot(p.astype(BF), ga_all, TN).astype(BF)
    grad_p = dot(ga_all, value, NT)
    inner = jnp.sum(p * grad_p, axis=-1, keepdims=True)
    gs[...] = (p * (grad_p - inner)).astype(BF)
    sum_o.across()
    cos, sin = cos_in[...], -sin_in[...]
    grad_q = dot(gs[...], key, NN) * scale
    for h in range(heads):
        gpre[:, h * head_dim : (h + 1) * head_dim] = turn(grad_q[h * seq : (h + 1) * seq], cos, sin).astype(BF)
    grad_k = dot(gs[...], q_rot[...].reshape(heads * seq, head_dim), TN) * scale
    gpre[:, heads * head_dim : (heads + 1) * head_dim] = turn(grad_k, cos, sin).astype(BF)
    gpre[:, (heads + 1) * head_dim :] = grad_value
    loads[1].wait()
    pre = gpre[...]
    in_part[...] = dot(pre, qkv_w[...].reshape((heads + 2) * head_dim, wide), NN).astype(BF)
    swap_y(3, in_part, in_got)
    swap_y(4, give.at[1], got.at[1])
    weight_grad(full_q, pre, lambda cols: nm_in[:, cols])
    sum_q.to_core()
    bias = jnp.sum(pre.astype(F32), axis=0, keepdims=True)
    sum_q.across()
    wires.landed(b_x, b_xrecv.at[0], at)
    b_acc[...] = out_cols[at.z].astype(F32) + b_x[...].astype(F32) + mid_half[...]
    out_line.close(b_acc)
    out_send[...] = b_acc[...].astype(BF)
    swap_y(5, out_send, out_got)
    out_tokens[at.t] = out_send[...]
    sum_o.along(go)
    wires.landed(in_got, y_recv.at[3], at)
    grad_in = in_part[...].astype(F32) + in_got[...].astype(F32)
    tok = tok_in[...].astype(F32)
    rms = lax.rsqrt(jnp.mean(tok * tok, axis=-1, keepdims=True) + EPS)
    unit = tok * rms
    grad_gain = jnp.sum(grad_in * unit, axis=0, keepdims=True)
    scaled = grad_in * gain_in[0:1]
    grad_tokens[...] = mid_low[...].reshape(seq, wide).astype(F32) + rms * (
        scaled - unit * jnp.mean(scaled * unit, axis=-1, keepdims=True)
    )
    wires.landed(gain_got, y_recv.at[1], at)
    gmlp = gain_part[...] + gain_got[...]
    lanes = small.shape[1]
    steps = wide // lanes
    for i in range(steps):
        small_all[at.dp, i : i + 1, :] = grad_gain[:, i * lanes : (i + 1) * lanes]
        small_all[at.dp, steps + i : steps + i + 1, :] = gmlp[:, i * lanes : (i + 1) * lanes]
    for i in range(bias.shape[1] // lanes):
        small_all[at.dp, 2 * steps + i : 2 * steps + i + 1, :] = bias[:, i * lanes : (i + 1) * lanes]
    for n, device in enumerate(others):
        wires.send(small_all.at[at.dp], small_all.at[at.dp], s_send.at[n], s_recv.at[at.dp], device)
    sum_q.along(gq)
    sum_o.close(go)
    sum_q.close(gq)
    for device in others:
        wires.landed(small_all.at[device[0]], s_recv.at[device[0]], at)
    total = small_all[0]
    for n in range(1, ndp):
        total = total + small_all[n]
    small[...] = total
    for i in range(2):
        wires.landed(got.at[i], y_recv.at[2 + 2 * i], at)
    wires.landed(out_got, y_recv.at[5], at)
    out_tokens[1 - at.t] = out_got[...]
    wires.drain()


def tail_step(nz, scale, out_cols, out_near, mid_half, grad_half, gain_part, att, q_rot, kv, probs, nm_in, tokens, gain, cos, sin, qkv, wo, give):
    ndp = 4 * nz
    half, wide = mid_half.shape
    seq = 2 * half
    heads, head_dim = wo.shape[:2]
    rows = head_dim // ndp
    shape = jax.ShapeDtypeStruct
    dma = pltpu.SemaphoreType.DMA
    vm = pltpu.VMEM
    lanes = wide // 3
    srows = 6 + (heads + 2) * head_dim // lanes
    return pl.pallas_call(
        functools.partial(tail_kernel, nz, scale),
        out_shape=(
            shape(((heads + 2) * rows, wide), F32),
            shape((heads * rows, wide), F32),
            shape((2, half, wide), BF),
            shape((seq, wide), F32),
            shape((srows, lanes), F32),
            shape(give.shape, BF),
        ),
        in_specs=[VM] * 14 + [ANY] * 3,
        out_specs=[VM] * 5 + [ANY],
        scratch_shapes=[
            vm((2, half, wide), BF),
            vm((1, wide), F32),
            vm(qkv.shape, BF),
            vm(wo.shape, BF),
            vm((heads + 2, head_dim, wide), F32),
            vm((heads, head_dim, wide), F32),
            vm((heads, seq, head_dim), BF),
            vm((heads * seq, seq), BF),
            vm((seq, (heads + 2) * head_dim), BF),
            vm((seq, wide), BF),
            vm((seq, wide), BF),
            vm((half, wide), BF),
            vm((nz, half, wide), BF),
            vm((half, wide), F32),
            vm((half, wide), BF),
            vm((half, wide), BF),
            vm((ndp, srows, lanes), F32),
            dma((2,)),
            dma((1,)),
            dma((1,)),
            dma((nz,)),
            dma((nz,)),
            dma((6,)),
            dma((6,)),
            dma((ndp,)),
            dma((ndp,)),
        ]
        + OwnerSum.buffers(nz, heads + 2, rows, wide)
        + OwnerSum.buffers(nz, heads, rows, wide)
        + OwnerSum.semaphores(nz)
        + OwnerSum.semaphores(nz),
        compiler_params=pltpu.CompilerParams(
            collective_id=3, has_side_effects=True, vmem_limit_bytes=VMEM_LIMIT
        ),
        name="tail_step",
    )(out_cols, out_near, mid_half, grad_half, gain_part, att, q_rot, kv, probs, nm_in, tokens, gain, cos, sin, qkv, wo, give)


def rope_tables(seq_len, head_dim):
    half_dim = head_dim // 2
    places = np.arange(seq_len, dtype=np.float32)
    freqs = np.float32(ROPE_BASE) ** (-(np.arange(half_dim, dtype=np.float32) * np.float32(2.0) / np.float32(head_dim)))
    angles = places[:, None] * freqs[None, :]
    cos, sin = np.cos(angles), np.sin(angles)
    return (
        jnp.asarray(np.concatenate([cos, cos], axis=1), F32),
        jnp.asarray(np.concatenate([-sin, sin], axis=1), F32),
    )


def planes(
    tokens,
    prefix,
    g_attn,
    w_query,
    b_query,
    w_key,
    b_key,
    w_value,
    b_value,
    w_out,
    g_mlp,
    w_gate,
    w_up,
    w_down,
    cotangent,
    ndp,
):
    nz = ndp // 4
    seq_len, wide = tokens.shape
    rows, heads = b_query.shape
    head_dim = rows * ndp
    dp = lax.axis_index("dp")
    gshare = g_attn.shape[0]

    def heads_first(w):
        return jnp.swapaxes(w, 0, 1)

    qkv_own = jnp.concatenate([heads_first(w_query), heads_first(w_key), heads_first(w_value)], axis=0)
    wo_own = heads_first(w_out)

    def row(v):
        flat = v.reshape(1, -1)
        return jnp.pad(flat, ((0, 0), (0, 128 - flat.shape[1])))

    def lay(v, count):
        return jnp.pad(v, ((0, count - v.shape[0]), (0, 128 - v.shape[1])))

    small_own = jnp.concatenate(
        [row(g_attn), lay(b_query.T, heads), lay(b_value.T, 8 - heads - 1), lay(g_mlp[None], 8)], axis=0
    )
    cos, sin = rope_tables(seq_len, head_dim)
    score_scale = head_dim ** (-0.5)
    att, q_rot, kv, probs, nm_in, gains, nm_half, mid_half, qkv_w, out_w, cot_all, mlp_all = attn_step(
        nz,
        score_scale,
        tokens,
        prefix,
        b_key.T.astype(F32),
        cos,
        sin,
        qkv_own,
        wo_own,
        small_own,
        cotangent,
        w_gate,
        w_up,
        w_down,
    )
    out_cols, out_near, keep_gate, keep_up, keep_down, give, grad_half, gain_part = mlp_step(
        nz, nm_half, mid_half, gains, cot_all, mlp_all, cotangent, w_gate, w_up, w_down
    )
    gq, go, out_tokens, grad_tokens, sums, got = tail_step(
        nz,
        score_scale,
        out_cols,
        out_near,
        mid_half,
        grad_half,
        gain_part,
        att,
        q_rot,
        kv,
        probs,
        nm_in,
        tokens,
        gains,
        cos,
        sin,
        qkv_w,
        out_w,
        give,
    )
    gq = gq.reshape(heads + 2, rows, wide).transpose(1, 0, 2)
    go = go.reshape(heads, rows, wide).transpose(1, 0, 2)
    gattn_all = sums[:3].reshape(wide)
    gmlp_all = sums[3:6].reshape(wide)
    bias_all = sums[6:].reshape(heads + 2, head_dim).T
    bias_own = lax.dynamic_slice_in_dim(bias_all, dp * rows, rows, axis=0)
    return (
        out_tokens.reshape(seq_len, wide),
        grad_tokens,
        lax.dynamic_slice_in_dim(gattn_all, dp * gshare, gshare),
        gq[:, :heads],
        bias_own[:, :heads],
        gq[:, heads : heads + 1],
        bias_all[:, heads : heads + 1],
        gq[:, heads + 1 :],
        bias_own[:, heads + 1 :],
        go,
        lax.dynamic_slice_in_dim(gmlp_all, dp * gshare, gshare),
        keep_gate + got[0].astype(F32),
        keep_up + got[1].astype(F32),
        keep_down,
    )


def local(*arrays, ndp):
    rows, heads = arrays[4].shape
    shard = arrays[11].shape[0]
    if ndp % 4 == 0 and rows % 8 == 0 and shard % 8 == 0 and heads <= 6 and arrays[6].shape[1] == 1:
        return planes(*arrays, ndp=ndp)
    return whole_gather(*arrays)


def solution(mesh):
    in_specs = (
        P("dp", None),
        P("dp"),
        P("dp"),
        P("dp", "tensor", None),
        P("dp", "tensor"),
        P("dp", "tensor", None),
        P(None, "tensor"),
        P("dp", "tensor", None),
        P("dp", "tensor"),
        P("dp", "tensor", None),
        P("dp"),
        P(("dp", "tensor"), None),
        P(("dp", "tensor"), None),
        P(("dp", "tensor"), None),
        P("dp", None),
    )
    out_specs = (
        P("dp", None),
        P("dp", None),
        P("dp"),
        P("dp", "tensor", None),
        P("dp", "tensor"),
        P("dp", "tensor", None),
        P(None, "tensor"),
        P("dp", "tensor", None),
        P("dp", "tensor"),
        P("dp", "tensor", None),
        P("dp"),
        P(("dp", "tensor"), None),
        P(("dp", "tensor"), None),
        P(("dp", "tensor"), None),
    )
    return jax.shard_map(functools.partial(local, ndp=mesh.shape["dp"]), mesh=mesh, in_specs=in_specs, out_specs=out_specs, check_vma=False)
```
